32 devices in a mesh: lon: 8 (over y, x, core), lat: 4 (over z).
Axes of the slice: x: 2, y: 2, z: 4, core: 2. Of those that a mesh axis runs over, the one named last changes fastest.
Arguments:
- increment: float32 [2, 137, 32, 1024], P(None, None, 'lat', 'lon'), may hold values from -6 to 6
- mixing: float32 [2, 137], replicated, may hold values from 0.02 to 0.12
- mixing_mask: int32 [32, 1024], P('lat', 'lon'), may hold values 0 or 1
- jacobian: bfloat16 [40, 20, 274], replicated, may hold values from -0.375 to 0.375
- fp_col: int32 [8, 4, 32], P('lon', 'lat'), may hold values from -1 to 1023, as said below
- fp_class: int32 [8, 4, 32], P('lon', 'lat'), may hold values from -1 to 39, as said below
- obs: float32 [8, 4, 20, 32], P('lon', 'lat'), may hold values from -6 to 6
- obs_weight: float32 [8, 4, 20, 32], P('lon', 'lat'), may hold values from 0.25 to 4
Outputs:
- gradient: float32 [2, 137, 32, 1024], P(None, None, 'lat', 'lon')
The draws below stay inside these ranges and needn't reach their ends.
Inputs may be any that keep to these rules, and one draw needn't show every extreme that they name: `fp_col`: -1 marks an empty slot; in each group of 8 slots from one tile to one owner the live slots come first; only owners with lat index a multiple of 1 have live slots; in every draw some group is full, and some owner is full from every source tile. `fp_class`: entry [l, d, s * 8 + k] is the class of the footprint in slot [l, s, d * 8 + k] of fp_col, and -1 exactly where that slot is empty.
All inputs are finite; a program needn't handle non-finite values. No bound on the sum of `mixing_mask` on one device may be relied on, other than what follows from the above.
Results may differ from the reference program's by a relative error of at most 0.00031.
Values may be sent and summed in bfloat16 or wider, within the bound.
A program may use at most 64 MiB of HBM per device.

```python
import math
import jax
import jax.numpy as jnp
from jax import lax

LEV = 137
CH = 20
NCLS = 40
CLAT = 8
CLON = 128
SLOT = 8
LEV2 = 274
COLS = 1024
TILES_LON = 8
TILES_LAT = 4
OWN_EVERY = 1
NLAT = 32
NLON = 1024


def slot_layout(key):
    base = jax.random.fold_in(key, 7001)
    key_count, key_src, key_dest, key_col, key_class = jax.random.split(base, 5)
    shape = (TILES_LON, TILES_LAT, TILES_LAT)
    counts = jax.random.randint(key_count, shape, max(1, SLOT // 3), SLOT + 1)
    full_src = jax.random.randint(key_src, (TILES_LON,), 0, TILES_LAT)
    full_dest = jax.random.randint(key_dest, (TILES_LON,), 0, TILES_LAT // OWN_EVERY) * OWN_EVERY
    index_src = jnp.arange(TILES_LAT)
    counts = jnp.where(index_src[None, :, None] == full_src[:, None, None], SLOT, counts)
    counts = jnp.where(index_src[None, None, :] == full_dest[:, None, None], SLOT, counts)
    counts = jnp.where((index_src % OWN_EVERY == 0)[None, None, :], counts, 0)
    is_live = jnp.arange(SLOT)[None, None, None, :] < counts[..., None]
    columns = jax.random.randint(key_col, shape + (SLOT,), 0, COLS)
    classes = jax.random.randint(key_class, shape + (SLOT,), 0, NCLS)
    return (is_live, columns, classes)


def draw_fp_col(key, part):
    is_live, columns, classes = slot_layout(key)
    picked = jnp.where(is_live, columns, -1)
    return picked.reshape(TILES_LON, TILES_LAT, TILES_LAT * SLOT).astype(jnp.int32)


def draw_fp_class(key, part):
    is_live, columns, classes = slot_layout(key)
    picked = jnp.where(is_live, classes, -1).transpose(0, 2, 1, 3)
    return picked.reshape(TILES_LON, TILES_LAT, TILES_LAT * SLOT).astype(jnp.int32)


def set_ends(result, rng, low, largest):
    extent = result.shape
    place = [jax.random.randint(jax.random.fold_in(rng, axis), (), 0, extent[axis]) for axis in range(len(extent))]
    result = result.at[tuple(place)].set(low)
    longest = extent.index(max(extent))
    place[longest] = (place[longest] + 1) % extent[longest]
    return result.at[tuple(place)].set(largest)


def block_scale(stream_key, dims, pieces, low, high):
    loudness = 1.0
    for dim, parts in pieces:
        steps = jax.random.uniform(jax.random.fold_in(jax.random.fold_in(stream_key, 6), dim), (parts,), jnp.float32, low / len(pieces), high / len(pieces))
        loudness = loudness * jnp.repeat(jnp.exp(steps), dims[dim] // parts).reshape((-1,) + (1,) * (len(dims) - 1 - dim))
    return loudness


def normal_values(key, shape, deviation, bound, cuts=(), held_as=jnp.bfloat16):
    factor_of = block_scale(key, shape, cuts, -0.22, 0.18) if cuts else 1.0
    array = jax.random.normal(key, shape, jnp.float32) * deviation * factor_of
    return jnp.minimum(jnp.maximum(array, -bound), bound).astype(held_as)


def setup_inputs(seed: int = 0) -> dict:
    key_of = jax.random.split(jax.random.key(seed), 9)
    increment = normal_values(key_of[0], (2, LEV, NLAT, NLON), 1.0, 6.0, ((2, 4), (3, 8)), jnp.float32)
    mixing = jnp.clip(jnp.exp(jax.random.uniform(key_of[1], (2, LEV), jnp.float32, math.log(0.02), math.log(0.12))), 0.02, 0.12)
    mixing_mask = set_ends((jax.random.randint(key_of[2], (NLAT, NLON), 0, 4) < 3).astype(jnp.int32), jax.random.fold_in(key_of[2], 1), 0, 1)
    jacobian = normal_values(key_of[3], (NCLS, CH, LEV2), LEV2 ** -0.5, 0.375)
    fp_col = draw_fp_col(jax.random.fold_in(key_of[8], 71), 0)
    fp_class = draw_fp_class(jax.random.fold_in(key_of[8], 71), 0)
    obs = normal_values(key_of[6], (TILES_LON, TILES_LAT, CH, TILES_LAT * SLOT), 1.0, 6.0, ((0, 8), (1, 4)), jnp.float32)
    obs_weight = jnp.clip(jnp.exp(math.log(4.0) - 2.7725887 * jax.random.uniform(key_of[7], (TILES_LON, TILES_LAT, CH, TILES_LAT * SLOT), jnp.float32) ** block_scale(key_of[7], (TILES_LON, TILES_LAT, CH, TILES_LAT * SLOT), ((0, 8), (1, 4)), -0.2, 0.2)), 0.25, 4.0)
    return dict(increment=increment, mixing=mixing, mixing_mask=mixing_mask, jacobian=jacobian, fp_col=fp_col, fp_class=fp_class, obs=obs, obs_weight=obs_weight)


def laplace(field):
    across = jnp.roll(field, 1, 3) + jnp.roll(field, -1, 3)
    padded = jnp.pad(field, ((0, 0), (0, 0), (1, 1), (0, 0)))
    return across + padded[:, :, 2:] + padded[:, :, :-2] - 4.0 * field


def reference(increment, mixing, mixing_mask, jacobian, fp_col, fp_class, obs, obs_weight):
    mix_scale = mixing[:, :, None, None] * mixing_mask.astype(jnp.float32)[None, None]
    advanced = increment + mix_scale * laplace(increment)
    state_bf = advanced.astype(jnp.bfloat16)
    tile_cols = state_bf.reshape(LEV2, TILES_LAT, CLAT, TILES_LON, CLON).transpose(3, 1, 0, 2, 4)
    tile_cols = tile_cols.reshape(TILES_LON * TILES_LAT, LEV2, COLS)
    slots = TILES_LAT * SLOT
    src_cols = fp_col.reshape(TILES_LON * TILES_LAT, slots)
    src_class = fp_class.reshape(TILES_LON, TILES_LAT, TILES_LAT, SLOT).transpose(0, 2, 1, 3)
    src_class = src_class.reshape(TILES_LON * TILES_LAT, slots)
    src_obs = obs.reshape(TILES_LON, TILES_LAT, CH, TILES_LAT, SLOT).transpose(0, 3, 2, 1, 4)
    src_obs = src_obs.reshape(TILES_LON * TILES_LAT, CH, slots)
    src_weight = obs_weight.reshape(TILES_LON, TILES_LAT, CH, TILES_LAT, SLOT).transpose(0, 3, 2, 1, 4)
    src_weight = src_weight.reshape(TILES_LON * TILES_LAT, CH, slots)

    def per_block(items):
        tile, wanted, classes, observed, weights = items
        is_live = wanted >= 0
        safe_col = jnp.maximum(wanted, 0).astype(jnp.int32)
        picked = jnp.take(tile, safe_col, axis=1).astype(jnp.float32) * is_live.astype(jnp.float32)[None]
        chosen = jacobian[jnp.maximum(classes, 0).astype(jnp.int32)].astype(jnp.float32)
        evolved = jnp.einsum("sck,ks->cs", chosen, picked)
        weighted = jnp.where(is_live[None], weights * (evolved - observed), 0.0).astype(jnp.bfloat16)
        adj_col = jnp.einsum("sck,cs->ks", chosen, weighted.astype(jnp.float32))
        return jnp.zeros((LEV2, COLS), jnp.float32).at[:, safe_col].add(adj_col)

    summed = lax.map(per_block, (tile_cols, src_cols, src_class, src_obs, src_weight))
    summed = summed.reshape(TILES_LON, TILES_LAT, LEV2, CLAT, CLON).transpose(2, 1, 3, 0, 4)
    summed = summed.reshape(2, LEV, NLAT, NLON)
    return increment + summed + laplace(mix_scale * summed)
```

```python
import functools

import jax
import jax.numpy as jnp
from jax import lax
from jax.experimental import pallas as pl
from jax.experimental.pallas import tpu as pltpu
from jax.sharding import PartitionSpec as P

MESH = pl.DeviceIdType.MESH
F32 = jnp.float32
BF16 = jnp.bfloat16
FAR = -1.0e6
NT = (((1,), (1,)), ((), ()))
NN = (((1,), (0,)), ((), ()))
TN = (((0,), (0,)), ((), ()))
LANES = 128


def dot(a, b, dims):
    return lax.dot_general(a, b, dims, preferred_element_type=F32)


def split(x):
    hi = x.astype(BF16)
    return hi, (x - hi.astype(F32)).astype(BF16)


def one(cond):
    return jnp.where(cond, 1.0, 0.0)


def cell_iota(slots, cells, row):
    lane = lax.broadcasted_iota(jnp.int32, (slots, cells), 1).astype(F32)
    return lane, lane + float(row * cells)


def laplace_row(q, slots, cells, row):
    lane, here = cell_iota(slots, cells, row)
    out = jnp.where(here == q, -4.0, 0.0)
    out += one((here == q + cells) | (here == q - cells))
    out += one((here == q + 1.0) & (lane != 0.0))
    out += one((here == q - 1.0) & (lane != cells - 1.0))
    return out


def columns_kernel(
    dims,
    inc_hbm, jac_hbm, mixing_ref, mask_ref, col_ref, cls_ref, obs_ref, wgt_ref,
    kmat_ref, qout_ref,
    inc, jac, jpad, xs, tsend, got, qs, lonsend, longot, latsend, latgot, msend, mgot,
    load_sem, t_send, t_recv, lon_send, lon_recv, lat_send, lat_recv, q_send, q_recv, m_send, m_recv,
):
    n_lon, n_lat, levels, rows, cells, slots, ncls, ch, chp = dims
    lon, lat = lax.axis_index("lon"), lax.axis_index("lat")
    per = slots // n_lat
    west, east = lax.rem(lon + n_lon - 1, n_lon), lax.rem(lon + 1, n_lon)
    has_north, has_south = lat > 0, lat < n_lat - 1

    load_inc = pltpu.make_async_copy(inc_hbm, inc, load_sem.at[0])
    load_jac = pltpu.make_async_copy(jac_hbm, jac, load_sem.at[1])
    load_inc.start()
    load_jac.start()

    barrier = pltpu.get_barrier_semaphore()
    for side in (west, east):
        pl.semaphore_signal(barrier, inc=1, device_id={"lon": side}, device_id_type=MESH)
    for k in range(1, n_lat):
        pl.semaphore_signal(
            barrier, inc=1, device_id={"lat": lax.rem(lat + k, n_lat)}, device_id_type=MESH
        )

    xs[...] = jnp.zeros_like(xs)
    for p in range(LANES // chp):
        xs[p * chp : p * chp + ch, 0:slots] = obs_ref[...]
        xs[LANES + p * chp : LANES + p * chp + ch, 0:slots] = wgt_ref[...]
    xs[2 * LANES :, 0:slots] = jnp.broadcast_to(cls_ref[...].astype(F32), (LANES, slots))
    for part in range(3):
        tsend[:, part * LANES : (part + 1) * LANES] = xs[part * LANES : (part + 1) * LANES, :].T[0:slots]
    qs[...] = jnp.full_like(qs, FAR)
    q_row = col_ref[...].astype(F32)
    qs[0:1, 0:slots] = jnp.where(q_row < 0.0, FAR, q_row)
    q_spread = jnp.broadcast_to(qs[0:1, :], (LANES, qs.shape[1])).T[0:slots]
    lonsend[...] = jnp.zeros_like(lonsend)
    qwide = qs.shape[1]
    lonsend[2 * rows :, 0:qwide] = qs[...]

    pl.semaphore_wait(barrier, 2 + n_lat - 1)

    t_copies = []
    for k in range(1, n_lat):
        s = lax.rem(lat + k, n_lat)
        copy = pltpu.make_async_remote_copy(
            src_ref=tsend.at[pl.ds(pl.multiple_of(s * per, per), per)],
            dst_ref=got.at[pl.ds(pl.multiple_of(lat * per, per), per)],
            send_sem=t_send.at[k - 1],
            recv_sem=t_recv.at[k - 1],
            device_id={"lat": s},
            device_id_type=MESH,
        )
        copy.start()
        t_copies.append(copy)
    own = pl.ds(pl.multiple_of(lat * per, per), per)
    got[own] = tsend[own]

    load_inc.wait()

    latsend[0] = inc[pl.ds(0, levels, stride=rows), :].astype(BF16)
    latsend[1] = inc[pl.ds(rows - 1, levels, stride=rows), :].astype(BF16)

    def to_lat(side, peer, src, dst, ss, rs):
        return pltpu.make_async_remote_copy(
            src_ref=src, dst_ref=dst, send_sem=ss, recv_sem=rs,
            device_id={"lat": peer}, device_id_type=MESH,
        )

    lat_peer = (jnp.maximum(lat - 1, 0), jnp.minimum(lat + 1, n_lat - 1))
    lat_has = (has_north, has_south)
    lat_copies = [
        to_lat(s, lat_peer[s], latsend.at[s], latgot.at[s], lat_send.at[s], lat_recv.at[s]) for s in (0, 1)
    ]
    for s in (0, 1):
        @pl.when(lat_has[s])
        def _(s=s):
            lat_copies[s].start()
        @pl.when(jnp.logical_not(lat_has[1 - s]))
        def _(s=s):
            latgot[s] = jnp.zeros_like(latgot[s])

    onehots, laps, edge_w, edge_e = [], [], [], []
    mask_f = jnp.zeros((slots, 1), F32)
    sub = lax.broadcasted_iota(jnp.int32, (rows, cells), 0)
    lane8 = lax.broadcasted_iota(jnp.int32, (rows, cells), 1)
    for r in range(rows):
        _, here = cell_iota(slots, cells, r)
        hot = one(here == q_spread)
        onehots.append(hot)
        laps.append(laplace_row(q_spread, slots, cells, r))
        edge_w.append(one((sub == r) & (lane8 == 0)))
        edge_e.append(one((sub == r) & (lane8 == cells - 1)))
    mask_f = sum(onehots[r] * mask_ref[r : r + 1, :].astype(F32) for r in range(rows))
    mask_f = jnp.sum(mask_f, axis=1, keepdims=True)
    picker = jnp.concatenate(
        [jnp.concatenate(part, axis=1) for part in (onehots, laps, edge_w, edge_e)], axis=0
    ).astype(BF16)
    field = jnp.concatenate([inc[pl.ds(r, levels, stride=rows), :] for r in range(rows)], axis=1)
    hi, lo = split(field)
    picked = dot(picker, hi, NT) + dot(picker, lo, NT)
    lonsend[0 : 2 * rows, 0:levels] = picked[2 * slots :]

    lon_copies = [
        pltpu.make_async_remote_copy(
            src_ref=lonsend, dst_ref=longot.at[s], send_sem=lon_send.at[s], recv_sem=lon_recv.at[s],
            device_id={"lon": peer}, device_id_type=MESH,
        )
        for s, peer in ((0, west), (1, east))
    ]
    for copy in lon_copies:
        copy.start()

    load_jac.wait()
    jpad[...] = jnp.zeros_like(jpad)
    for c in range(ncls):
        jpad[c * chp : c * chp + ch, :] = jac[c]

    mix_row = jnp.concatenate([mixing_ref[0:1, :], mixing_ref[1:2, :]], axis=1)
    scale = mix_row * mask_f

    lane_s = lax.broadcasted_iota(jnp.int32, (slots, cells), 1).astype(F32)
    lane_r = lax.broadcasted_iota(jnp.int32, (slots, rows), 1).astype(F32)
    q_rows = q_spread[:, 0:rows]
    hot_w = one(q_rows == lane_r * cells).astype(BF16)
    hot_e = one(q_rows == lane_r * cells + (cells - 1)).astype(BF16)
    hot_n = one(q_spread == lane_s).astype(BF16)
    hot_s = one(q_spread == lane_s + float((rows - 1) * cells)).astype(BF16)

    for s in (0, 1):
        @pl.when(lat_has[1 - s])
        def _(s=s):
            lat_copies[s].wait_recv()
    halo = dot(hot_s, latgot[0], NT) + dot(hot_n, latgot[1], NT)
    for copy in lon_copies:
        copy.wait_recv()
    halo += dot(hot_e, longot[0, 0:rows, 0:levels].astype(BF16), NN)
    halo += dot(hot_w, longot[1, rows : 2 * rows, 0:levels].astype(BF16), NN)
    columns = (picked[0:slots] + scale * (picked[slots : 2 * slots] + halo)).astype(BF16)
    evolved = dot(columns, jpad[...], NT)
    for copy in t_copies:
        copy.wait_recv()
    observed, weight, cls = (got[:, p * LANES : (p + 1) * LANES] for p in range(3))
    lane_i = lax.broadcasted_iota(jnp.int32, (slots, LANES), 1)
    group = sum(one(lane_i >= p * chp) for p in range(1, LANES // chp))
    parts = []
    for t in range(ncls * chp // LANES):
        w = weight * (evolved[:, t * LANES : (t + 1) * LANES] - observed)
        parts.append(jnp.where(cls == group + float(t * (LANES // chp)), w, 0.0).astype(BF16))
    spread = jnp.concatenate(parts, axis=1)
    adj = dot(spread, jpad[...], NN)
    madj = scale * adj
    mhi, mlo = split(madj)
    msend[:, 0:levels] = mhi

    m_copies = []
    for s in (0, 1):
        copy = pltpu.make_async_remote_copy(
            src_ref=msend, dst_ref=mgot.at[s], send_sem=m_send.at[s], recv_sem=m_recv.at[s],
            device_id={"lon": (west, east)[s]}, device_id_type=MESH,
        )
        copy.start()
        m_copies.append(copy)
    ml_copies, ql_copies = [], []
    for s in (0, 1):
        ml_copies.append(to_lat(s, lat_peer[s], msend, mgot.at[2 + s], m_send.at[2 + s], m_recv.at[2 + s]))
        ql_copies.append(to_lat(s, lat_peer[s], lonsend, longot.at[2 + s], q_send.at[s], q_recv.at[s]))

        @pl.when(lat_has[s])
        def _(s=s):
            ml_copies[s].start()
            ql_copies[s].start()

        @pl.when(jnp.logical_not(lat_has[1 - s]))
        def _(s=s):
            mgot[2 + s] = jnp.zeros_like(mgot[2 + s])
            longot[2 + s, 2 * rows :, 0:qwide] = jnp.full((qs.shape[0], qwide), FAR, F32)

    ahi, alo = split(adj)
    kmat_ref[0:slots] = ahi
    kmat_ref[slots : 2 * slots] = alo
    kmat_ref[2 * slots : 3 * slots] = mhi
    kmat_ref[3 * slots : 4 * slots] = mlo
    qout_ref[0] = qs[...]

    for copy in t_copies + lon_copies + m_copies:
        copy.wait_send()
    for s in (0, 1):
        @pl.when(lat_has[s])
        def _(s=s):
            lat_copies[s].wait_send()
            ml_copies[s].wait_send()
            ql_copies[s].wait_send()

        @pl.when(lat_has[1 - s])
        def _(s=s):
            ml_copies[s].wait_recv()
            ql_copies[s].wait_recv()
    for copy in m_copies:
        copy.wait_recv()
    for i in range(4):
        kmat_ref[(4 + i) * slots : (5 + i) * slots] = mgot[i, :, 0:levels]
        qout_ref[1 + i] = longot[i, 2 * rows :, 0:qwide]


def gradient_kernel(dims, chunks, kmat_ref, q_ref, inc_hbm, out_hbm, inc, out, in_sem, out_sem):
    n_lon, n_lat, levels, rows, cells, slots, ncls, ch, chp = dims
    loads, stores = [], []
    for i, (at, size) in enumerate(chunks):
        span = pl.ds(at * rows, size * rows)
        loads.append(pltpu.make_async_copy(inc_hbm.at[span], inc.at[span], in_sem.at[i]))
        stores.append(pltpu.make_async_copy(out.at[span], out_hbm.at[span], out_sem.at[i]))
        loads[i].start()
    q = [jnp.broadcast_to(q_ref[i, 0:1, :], (LANES, q_ref.shape[2])).T[0:slots] for i in range(5)]
    hots = []
    span = float(cells * (rows - 1))
    for r in range(rows):
        lane, here = cell_iota(slots, cells, r)
        hot = one(here == q[0]).astype(BF16)
        lap = laplace_row(q[0], slots, cells, r).astype(BF16)
        east = one((here == q[1] + (cells - 1.0)) & (lane == cells - 1.0)).astype(BF16)
        west = one((here == q[2] - (cells - 1.0)) & (lane == 0.0)).astype(BF16)
        south = one(here == q[3] + span).astype(BF16)
        north = one(here == q[4] - span).astype(BF16)
        hots.append(jnp.concatenate([hot, hot, lap, lap, east, west, south, north], axis=0))
    hots = jnp.concatenate(hots, axis=1)
    total = dot(kmat_ref[...], hots, TN)
    for i, (at, size) in enumerate(chunks):
        loads[i].wait()
        for r in range(rows):
            span = pl.ds(at * rows + r, size, stride=rows)
            out[span, :] = inc[span, :] + total[at : at + size, r * cells : (r + 1) * cells]
        stores[i].start()
    for store in stores:
        store.wait()


def round_up(x, m):
    return -(-x // m) * m


def on_device(n_lon, n_lat, increment, mixing, mixing_mask, jacobian, fp_col, fp_class, obs, obs_weight):
    nvar, lev, rows, cells = increment.shape
    levels = nvar * lev
    ncls, ch, _ = jacobian.shape
    slots = fp_col.shape[-1]
    chp = round_up(ch, 16)
    dims = (n_lon, n_lat, levels, rows, cells, slots, ncls, ch, chp)
    qwide = round_up(slots, LANES)
    wide = max(round_up(levels, LANES), qwide)
    flat = increment.reshape(levels * rows, cells)
    vmem = pl.BlockSpec(memory_space=pltpu.VMEM)
    hbm = pl.BlockSpec(memory_space=pl.ANY)
    dma = pltpu.SemaphoreType.DMA
    kmat, q = pl.pallas_call(
        functools.partial(columns_kernel, dims),
        out_shape=(
            jax.ShapeDtypeStruct((8 * slots, levels), BF16),
            jax.ShapeDtypeStruct((5, 8, qwide), F32),
        ),
        in_specs=[hbm, hbm] + [vmem] * 6,
        out_specs=(vmem, vmem),
        scratch_shapes=[
            pltpu.VMEM((levels * rows, cells), F32),
            pltpu.VMEM(jacobian.shape, BF16),
            pltpu.VMEM((ncls * chp, levels), BF16),
            pltpu.VMEM((3 * LANES, qwide), F32),
            pltpu.VMEM((slots, 3 * LANES), F32),
            pltpu.VMEM((slots, 3 * LANES), F32),
            pltpu.VMEM((8, qwide), F32),
            pltpu.VMEM((2 * rows + 8, wide), F32),
            pltpu.VMEM((4, 2 * rows + 8, wide), F32),
            pltpu.VMEM((2, levels, cells), BF16),
            pltpu.VMEM((2, levels, cells), BF16),
            pltpu.VMEM((slots, round_up(levels, LANES)), BF16),
            pltpu.VMEM((4, slots, round_up(levels, LANES)), BF16),
            dma((2,)),
            dma((n_lat - 1,)),
            dma((n_lat - 1,)),
            dma((2,)),
            dma((2,)),
            dma((2,)),
            dma((2,)),
            dma((2,)),
            dma((2,)),
            dma((4,)),
            dma((4,)),
        ],
        compiler_params=pltpu.CompilerParams(collective_id=0, has_side_effects=True),
        name="columns",
    )(
        flat, jacobian, mixing, mixing_mask, fp_col[0], fp_class[0], obs[0, 0], obs_weight[0, 0]
    )
    step = 8 * pl.cdiv(levels, 24)
    chunks = [(at, min(step, levels - at)) for at in range(0, levels, step)]
    out = pl.pallas_call(
        functools.partial(gradient_kernel, dims, chunks),
        out_shape=jax.ShapeDtypeStruct(flat.shape, F32),
        in_specs=[vmem, vmem, hbm],
        out_specs=hbm,
        scratch_shapes=[
            pltpu.VMEM(flat.shape, F32),
            pltpu.VMEM(flat.shape, F32),
            dma((len(chunks),)),
            dma((len(chunks),)),
        ],
        name="gradient",
    )(kmat, q, flat)
    return out.reshape(increment.shape)


def solution(mesh):
    return jax.shard_map(
        functools.partial(on_device, mesh.shape["lon"], mesh.shape["lat"]),
        mesh=mesh,
        in_specs=(
            P(None, None, "lat", "lon"),
            P(),
            P("lat", "lon"),
            P(),
            P("lon", "lat", None),
            P("lon", "lat", None),
            P("lon", "lat", None, None),
            P("lon", "lat", None, None),
        ),
        out_specs=P(None, None, "lat", "lon"),
        check_vma=False,
    )
```

```python
import functools

import jax
import jax.numpy as jnp
from jax import lax
from jax.experimental import pallas as pl
from jax.experimental.pallas import tpu as pltpu
from jax.sharding import PartitionSpec as P

MESH = pl.DeviceIdType.MESH
F32 = jnp.float32
BF16 = jnp.bfloat16
FAR = -1.0e6
NT = (((1,), (1,)), ((), ()))
NN = (((1,), (0,)), ((), ()))
TN = (((0,), (0,)), ((), ()))
LANES = 128
VMEM_LIMIT = 40 << 20


def dot(a, b, dims):
    return lax.dot_general(a, b, dims, preferred_element_type=F32)


def split(x):
    hi = x.astype(BF16)
    return hi, (x - hi.astype(F32)).astype(BF16)


def one(cond):
    return jnp.where(cond, 1.0, 0.0)


def cell_iota(slots, cells, row):
    lane = lax.broadcasted_iota(jnp.int32, (slots, cells), 1).astype(F32)
    return lane, lane + float(row * cells)


def laplace_row(q, slots, cells, row):
    lane, here = cell_iota(slots, cells, row)
    out = jnp.where(here == q, -4.0, 0.0)
    out += one((here == q + cells) | (here == q - cells))
    out += one((here == q + 1.0) & (lane != 0.0))
    out += one((here == q - 1.0) & (lane != cells - 1.0))
    return out


def columns_kernel(
    dims,
    inc_hbm, jac_hbm, mixing_hbm, mask_hbm, col_hbm, cls_hbm, obs_hbm, wgt_hbm,
    out,
    inc, jac, mixing, mask, col, cls_in, obs, wgt,
    xs, tsend, got, qs, qgot, lonsend, longot, latsend, latgot, msend, mgot,
    load_sem, t_send, t_recv, lon_send, lon_recv, lat_send, lat_recv, q_send, q_recv, m_send, m_recv,
):
    n_lon, n_lat, levels, rows, cells, slots, ncls, ch, chp = dims
    lon, lat = lax.axis_index("lon"), lax.axis_index("lat")
    per = slots // n_lat
    width = ncls * ch
    west, east = lax.rem(lon + n_lon - 1, n_lon), lax.rem(lon + 1, n_lon)
    lat_has = (lat > 0, lat < n_lat - 1)
    lat_peer = (jnp.maximum(lat - 1, 0), jnp.minimum(lat + 1, n_lat - 1))

    loads = [
        pltpu.make_async_copy(a, b, load_sem.at[i])
        for i, (a, b) in enumerate(
            (
                (inc_hbm, inc), (col_hbm, col), (cls_hbm, cls_in), (obs_hbm, obs),
                (wgt_hbm, wgt), (mask_hbm, mask), (mixing_hbm, mixing), (jac_hbm, jac),
            )
        )
    ]
    barrier = pltpu.get_barrier_semaphore()
    for k in range(1, n_lat):
        pl.semaphore_signal(
            barrier, inc=1, device_id={"lat": lax.rem(lat + k, n_lat)}, device_id_type=MESH
        )
    for side in (west, east):
        pl.semaphore_signal(barrier, inc=1, device_id={"lon": side}, device_id_type=MESH)
    for load in loads:
        load.start()

    for load in loads[1:7]:
        load.wait()
    xs[...] = jnp.zeros_like(xs)
    xs[0:ch, 0:slots] = obs[:, 0, :]
    xs[chp : chp + ch, 0:slots] = wgt[:, 0, :]
    xs[2 * chp : 2 * chp + 1, 0:slots] = cls_in[...].astype(F32)
    tsend[...] = xs[...].T[0:slots]
    qs[...] = jnp.full_like(qs, FAR)
    q_row = col[...].astype(F32)
    qs[0:1, 0:slots] = jnp.where(q_row < 0.0, FAR, q_row)
    q_spread = jnp.broadcast_to(qs[0:1, :], (LANES, qs.shape[1])).T[0:slots]

    onehots, laps, edge_w, edge_e = [], [], [], []
    sub = lax.broadcasted_iota(jnp.int32, (rows, cells), 0)
    lane8 = lax.broadcasted_iota(jnp.int32, (rows, cells), 1)
    mask_f = jnp.zeros((slots, cells), F32)
    for r in range(rows):
        _, here = cell_iota(slots, cells, r)
        hot = one(here == q_spread)
        mask_f += hot * mask[r : r + 1, :].astype(F32)
        onehots.append(hot)
        laps.append(laplace_row(q_spread, slots, cells, r))
        edge_w.append(one((sub == r) & (lane8 == 0)))
        edge_e.append(one((sub == r) & (lane8 == cells - 1)))
    mask_f = jnp.sum(mask_f, axis=1, keepdims=True)
    hot, lap = (jnp.concatenate(part, axis=1).astype(BF16) for part in (onehots, laps))
    edges = jnp.concatenate(
        [jnp.concatenate(part, axis=1) for part in (edge_w, edge_e)], axis=0
    ).astype(BF16)
    mix_row = jnp.concatenate([mixing[0:1, :], mixing[1:2, :]], axis=1)
    scale = mix_row * mask_f

    loads[0].wait()
    latsend[0] = inc[pl.ds(0, levels, stride=rows), :].astype(BF16)
    latsend[1] = inc[pl.ds(rows - 1, levels, stride=rows), :].astype(BF16)
    field = jnp.concatenate([inc[pl.ds(r, levels, stride=rows), :] for r in range(rows)], axis=1)
    hi, lo = split(field)
    picked = dot(jnp.concatenate([hot, lap, edges], axis=0), hi, NT)
    lonsend[:, 0:levels] = picked[2 * slots :].astype(BF16)
    picked = picked[0 : 2 * slots] + dot(jnp.concatenate([hot, lap], axis=0), lo, NT)

    pl.semaphore_wait(barrier, 2 + n_lat - 1)

    t_copies = []
    for k in range(1, n_lat):
        s = lax.rem(lat + k, n_lat)
        copy = pltpu.make_async_remote_copy(
            src_ref=tsend.at[pl.ds(pl.multiple_of(s * per, per), per)],
            dst_ref=got.at[pl.ds(pl.multiple_of(lat * per, per), per)],
            send_sem=t_send.at[k - 1], recv_sem=t_recv.at[k - 1],
            device_id={"lat": s}, device_id_type=MESH,
        )
        copy.start()
        t_copies.append(copy)

    def to(peer, src, dst, ss, rs):
        return pltpu.make_async_remote_copy(
            src_ref=src, dst_ref=dst, send_sem=ss, recv_sem=rs, device_id=peer, device_id_type=MESH
        )

    peers = ({"lon": west}, {"lon": east}, {"lat": lat_peer[0]}, {"lat": lat_peer[1]})
    lon_copies = [to(peers[s], lonsend, longot.at[s], lon_send.at[s], lon_recv.at[s]) for s in (0, 1)]
    lat_copies = [to(peers[2 + s], latsend.at[s], latgot.at[s], lat_send.at[s], lat_recv.at[s]) for s in (0, 1)]
    q_copies = [to(peers[s], qs, qgot.at[s], q_send.at[s], q_recv.at[s]) for s in range(4)]
    m_copies = [to(peers[s], msend, mgot.at[s], m_send.at[s], m_recv.at[s]) for s in range(4)]
    for copy in lon_copies:
        copy.start()
    for s in (0, 1):
        @pl.when(lat_has[s])
        def _(s=s):
            lat_copies[s].start()
    for copy in q_copies[0:2]:
        copy.start()
    for s in (0, 1):
        @pl.when(lat_has[s])
        def _(s=s):
            q_copies[2 + s].start()

        @pl.when(jnp.logical_not(lat_has[1 - s]))
        def _(s=s):
            latgot[s] = jnp.zeros_like(latgot[s])
            mgot[2 + s] = jnp.zeros_like(mgot[2 + s])
            qgot[2 + s] = jnp.full((qs.shape[0], qs.shape[1]), FAR, F32)

    own = pl.ds(pl.multiple_of(lat * per, per), per)
    got[own] = tsend[own]

    lane_s = lax.broadcasted_iota(jnp.int32, (slots, cells), 1).astype(F32)
    lane_r = lax.broadcasted_iota(jnp.int32, (slots, rows), 1).astype(F32)
    q_rows = q_spread[:, 0:rows]
    hot_w = one(q_rows == lane_r * cells).astype(BF16)
    hot_e = one(q_rows == lane_r * cells + (cells - 1)).astype(BF16)
    hot_n = one(q_spread == lane_s).astype(BF16)
    hot_s = one(q_spread == lane_s + float((rows - 1) * cells)).astype(BF16)
    lane_i = lax.broadcasted_iota(jnp.int32, (1, width), 1).astype(F32)
    lane_ch = jnp.floor((lane_i + 0.5) * (1.0 / ncls))
    lane_cls = lane_i - lane_ch * ncls
    sub_k = lax.broadcasted_iota(jnp.int32, (LANES, width), 0).astype(F32)
    at_obs = one(sub_k == lane_ch).astype(BF16)
    at_wgt = one(sub_k == lane_ch + float(chp)).astype(BF16)
    at_obs = jnp.concatenate([at_obs, at_obs], axis=0)
    at_wgt = jnp.concatenate([at_wgt, at_wgt], axis=0)

    loads[7].wait()
    for copy in lon_copies:
        copy.wait_recv()
    halo = dot(hot_e, longot[0, 0:rows, 0:levels], NN)
    halo += dot(hot_w, longot[1, rows : 2 * rows, 0:levels], NN)
    for copy in t_copies:
        copy.wait_recv()
    told = got[...]
    thi, tlo = split(told)
    told2 = jnp.concatenate([thi, tlo], axis=1)
    observed = dot(told2, at_obs, NN)
    weight = dot(told2, at_wgt, NN)
    mine = jnp.broadcast_to(told[:, 2 * chp : 2 * chp + 1], (slots, width)) == lane_cls
    for s in (0, 1):
        @pl.when(lat_has[1 - s])
        def _(s=s):
            lat_copies[s].wait_recv()
    halo += dot(hot_s, latgot[0], NT) + dot(hot_n, latgot[1], NT)
    columns = (picked[0:slots] + scale * (picked[slots : 2 * slots] + halo)).astype(BF16)
    evolved = dot(columns, jac[...], NT)
    spread = jnp.where(mine, weight * (evolved - observed), 0.0).astype(BF16)
    adj = dot(spread, jac[...], NN)
    mhi, mlo = split(scale * adj)
    msend[:, 0:levels] = mhi
    for copy in m_copies[0:2]:
        copy.start()
    for s in (0, 1):
        @pl.when(lat_has[s])
        def _(s=s):
            m_copies[2 + s].start()

    ahi, alo = split(adj)
    total = dot(
        jnp.concatenate([ahi, alo, mhi, mlo], axis=0), jnp.concatenate([hot, hot, lap, lap], axis=0), TN
    )
    for r in range(rows):
        span = pl.ds(r, levels, stride=rows)
        out[span, :] = inc[span, :] + total[:, r * cells : (r + 1) * cells]

    for copy in q_copies[0:2]:
        copy.wait_recv()
    for s in (0, 1):
        @pl.when(lat_has[1 - s])
        def _(s=s):
            q_copies[2 + s].wait_recv()
    q = [jnp.broadcast_to(qgot[i, 0:1, :], (LANES, qs.shape[1])).T[0:slots] for i in range(4)]
    nearby = []
    for r in range(rows):
        lane, here = cell_iota(slots, cells, r)
        zero = jnp.zeros((slots, cells), F32)
        nearby.append(
            jnp.concatenate(
                [
                    one((here == q[0] + (cells - 1.0)) & (lane == cells - 1.0)),
                    one((here == q[1] - (cells - 1.0)) & (lane == 0.0)),
                    one(lane == q[2]) if r == rows - 1 else zero,
                    one(lane == q[3] - float(cells * (rows - 1))) if r == 0 else zero,
                ],
                axis=0,
            ).astype(BF16)
        )
    nearby = jnp.concatenate(nearby, axis=1)
    for copy in m_copies[0:2]:
        copy.wait_recv()
    for s in (0, 1):
        @pl.when(lat_has[1 - s])
        def _(s=s):
            m_copies[2 + s].wait_recv()
    total = dot(jnp.concatenate([mgot[i, :, 0:levels] for i in range(4)], axis=0), nearby, TN)
    for r in range(rows):
        span = pl.ds(r, levels, stride=rows)
        out[span, :] += total[:, r * cells : (r + 1) * cells]

    for copy in t_copies + lon_copies + q_copies[0:2] + m_copies[0:2]:
        copy.wait_send()
    for s in (0, 1):
        @pl.when(lat_has[s])
        def _(s=s):
            lat_copies[s].wait_send()
            q_copies[2 + s].wait_send()
            m_copies[2 + s].wait_send()


def round_up(x, m):
    return -(-x // m) * m


def on_device(n_lon, n_lat, increment, mixing, mixing_mask, jacobian, fp_col, fp_class, obs, obs_weight):
    nvar, lev, rows, cells = increment.shape
    levels = nvar * lev
    ncls, ch, _ = jacobian.shape
    slots = fp_col.shape[-1]
    chp = round_up(ch, 16)
    dims = (n_lon, n_lat, levels, rows, cells, slots, ncls, ch, chp)
    qwide = round_up(slots, LANES)
    wide = round_up(levels, LANES)
    args = (
        increment.reshape(levels * rows, cells),
        jnp.transpose(jacobian, (1, 0, 2)).reshape(ch * ncls, levels),
        mixing,
        mixing_mask,
        fp_col[0],
        fp_class[0],
        obs.transpose(2, 0, 1, 3).reshape(ch, 1, slots),
        obs_weight.transpose(2, 0, 1, 3).reshape(ch, 1, slots),
    )
    dma = pltpu.SemaphoreType.DMA
    out = pl.pallas_call(
        functools.partial(columns_kernel, dims),
        out_shape=jax.ShapeDtypeStruct((levels * rows, cells), F32),
        in_specs=[pl.BlockSpec(memory_space=pltpu.MemorySpace.HBM)] * len(args),
        out_specs=pl.BlockSpec(memory_space=pltpu.VMEM),
        scratch_shapes=[pltpu.VMEM(a.shape, a.dtype) for a in args]
        + [
            pltpu.VMEM((LANES, qwide), F32),
            pltpu.VMEM((slots, LANES), F32),
            pltpu.VMEM((slots, LANES), F32),
            pltpu.VMEM((8, qwide), F32),
            pltpu.VMEM((4, 8, qwide), F32),
            pltpu.VMEM((2 * rows, wide), BF16),
            pltpu.VMEM((2, 2 * rows, wide), BF16),
            pltpu.VMEM((2, levels, cells), BF16),
            pltpu.VMEM((2, levels, cells), BF16),
            pltpu.VMEM((slots, wide), BF16),
            pltpu.VMEM((4, slots, wide), BF16),
            dma((len(args),)),
            dma((n_lat - 1,)),
            dma((n_lat - 1,)),
        ]
        + [dma((n,)) for n in (2, 2, 2, 2, 4, 4, 4, 4)],
        compiler_params=pltpu.CompilerParams(
            collective_id=0, has_side_effects=True, vmem_limit_bytes=VMEM_LIMIT
        ),
        name="columns",
    )(*args)
    return out.reshape(increment.shape)


def solution(mesh):
    return jax.shard_map(
        functools.partial(on_device, mesh.shape["lon"], mesh.shape["lat"]),
        mesh=mesh,
        in_specs=(
            P(None, None, "lat", "lon"),
            P(),
            P("lat", "lon"),
            P(),
            P("lon", "lat", None),
            P("lon", "lat", None),
            P("lon", "lat", None, None),
            P("lon", "lat", None, None),
        ),
        out_specs=P(None, None, "lat", "lon"),
        check_vma=False,
    )
```

```python
import functools

import jax
import jax.numpy as jnp
from jax import lax
from jax.experimental import pallas as pl
from jax.experimental.pallas import tpu as pltpu
from jax.sharding import PartitionSpec as P

MESH = pl.DeviceIdType.MESH
F32 = jnp.float32
BF16 = jnp.bfloat16
FAR = -1.0e6
NT = (((1,), (1,)), ((), ()))
NN = (((1,), (0,)), ((), ()))
TN = (((0,), (0,)), ((), ()))
LANES = 128
VMEM_LIMIT = 40 << 20


def dot(a, b, dims):
    return lax.dot_general(a, b, dims, preferred_element_type=F32)


def split(x):
    hi = x.astype(BF16)
    return hi, (x - hi.astype(F32)).astype(BF16)


def one(cond):
    return jnp.where(cond, 1.0, 0.0)


def cell_iota(slots, cells, row):
    lane = lax.broadcasted_iota(jnp.int32, (slots, cells), 1).astype(F32)
    return lane, lane + float(row * cells)


def laplace_row(q, slots, cells, row):
    lane, here = cell_iota(slots, cells, row)
    out = jnp.where(here == q, -4.0, 0.0)
    out += one((here == q + cells) | (here == q - cells))
    out += one((here == q + 1.0) & (lane != 0.0))
    out += one((here == q - 1.0) & (lane != cells - 1.0))
    return out


def columns_kernel(
    dims,
    inc_hbm, jac_hbm, mixing_hbm, mask_hbm, col_hbm, cls_hbm, obs_hbm, wgt_hbm,
    out,
    inc, jac, mixing, mask, col, cls_in, obs, wgt,
    xs, tsend, got, qs, qgot, lonsend, longot, latsend, latgot, msend, mgot,
    load_sem, t_send, t_recv, lon_send, lon_recv, lat_send, lat_recv, q_send, q_recv, m_send, m_recv,
):
    n_lon, n_lat, levels, rows, cells, slots, ncls, ch, chp = dims
    lon, lat = lax.axis_index("lon"), lax.axis_index("lat")
    per = slots // n_lat
    width = ncls * ch
    west, east = lax.rem(lon + n_lon - 1, n_lon), lax.rem(lon + 1, n_lon)
    lat_has = (lat > 0, lat < n_lat - 1)
    lat_peer = (jnp.maximum(lat - 1, 0), jnp.minimum(lat + 1, n_lat - 1))

    loads = [
        pltpu.make_async_copy(a, b, load_sem.at[i])
        for i, (a, b) in enumerate(
            (
                (inc_hbm, inc), (col_hbm, col), (cls_hbm, cls_in), (obs_hbm, obs),
                (wgt_hbm, wgt), (mask_hbm, mask), (mixing_hbm, mixing), (jac_hbm, jac),
            )
        )
    ]
    barrier = pltpu.get_barrier_semaphore()
    for k in range(1, n_lat):
        pl.semaphore_signal(
            barrier, inc=1, device_id={"lat": lax.rem(lat + k, n_lat)}, device_id_type=MESH
        )
    for side in (west, east):
        pl.semaphore_signal(barrier, inc=1, device_id={"lon": side}, device_id_type=MESH)
    for load in loads:
        load.start()

    for load in loads[1:7]:
        load.wait()
    xs[...] = jnp.zeros_like(xs)
    xs[0:ch, 0:slots] = obs[:, 0, :]
    xs[chp : chp + ch, 0:slots] = wgt[:, 0, :]
    xs[2 * chp : 2 * chp + 1, 0:slots] = cls_in[...].astype(F32)
    tsend[...] = xs[...].T[0:slots]
    qs[...] = jnp.full_like(qs, FAR)
    q_row = col[...].astype(F32)
    qs[0:1, 0:slots] = jnp.where(q_row < 0.0, FAR, q_row)
    q_spread = jnp.broadcast_to(qs[0:1, :], (LANES, qs.shape[1])).T[0:slots]

    onehots, laps, edge_w, edge_e = [], [], [], []
    sub = lax.broadcasted_iota(jnp.int32, (rows, cells), 0)
    lane8 = lax.broadcasted_iota(jnp.int32, (rows, cells), 1)
    mask_f = jnp.zeros((slots, cells), F32)
    for r in range(rows):
        _, here = cell_iota(slots, cells, r)
        hot = one(here == q_spread)
        mask_f += hot * mask[r : r + 1, :].astype(F32)
        onehots.append(hot)
        laps.append(laplace_row(q_spread, slots, cells, r))
        edge_w.append(one((sub == r) & (lane8 == 0)))
        edge_e.append(one((sub == r) & (lane8 == cells - 1)))
    mask_f = jnp.sum(mask_f, axis=1, keepdims=True)
    hot, lap = (jnp.concatenate(part, axis=1).astype(BF16) for part in (onehots, laps))
    edges = jnp.concatenate(
        [jnp.concatenate(part, axis=1) for part in (edge_w, edge_e)], axis=0
    ).astype(BF16)
    mix_row = jnp.concatenate([mixing[0:1, :], mixing[1:2, :]], axis=1)
    scale = mix_row * mask_f

    loads[0].wait()
    latsend[0] = inc[pl.ds(0, levels, stride=rows), :].astype(BF16)
    latsend[1] = inc[pl.ds(rows - 1, levels, stride=rows), :].astype(BF16)
    field = jnp.concatenate([inc[pl.ds(r, levels, stride=rows), :] for r in range(rows)], axis=1)
    hi, lo = split(field)
    picked = dot(jnp.concatenate([hot, lap, edges], axis=0), hi, NT)
    lonsend[:, 0:levels] = picked[2 * slots :].astype(BF16)
    picked = picked[0 : 2 * slots] + dot(jnp.concatenate([hot, lap], axis=0), lo, NT)

    pl.semaphore_wait(barrier, 2 + n_lat - 1)

    t_copies = []
    for k in range(1, n_lat):
        s = lax.rem(lat + k, n_lat)
        copy = pltpu.make_async_remote_copy(
            src_ref=tsend.at[pl.ds(pl.multiple_of(s * per, per), per)],
            dst_ref=got.at[pl.ds(pl.multiple_of(lat * per, per), per)],
            send_sem=t_send.at[k - 1], recv_sem=t_recv.at[k - 1],
            device_id={"lat": s}, device_id_type=MESH,
        )
        copy.start()
        t_copies.append(copy)

    def to(peer, src, dst, ss, rs):
        return pltpu.make_async_remote_copy(
            src_ref=src, dst_ref=dst, send_sem=ss, recv_sem=rs, device_id=peer, device_id_type=MESH
        )

    peers = ({"lon": west}, {"lon": east}, {"lat": lat_peer[0]}, {"lat": lat_peer[1]})
    lon_copies = [to(peers[s], lonsend, longot.at[s], lon_send.at[s], lon_recv.at[s]) for s in (0, 1)]
    lat_copies = [to(peers[2 + s], latsend.at[s], latgot.at[s], lat_send.at[s], lat_recv.at[s]) for s in (0, 1)]
    q_copies = [to(peers[s], qs, qgot.at[s], q_send.at[s], q_recv.at[s]) for s in range(4)]
    m_copies = [to(peers[s], msend, mgot.at[s], m_send.at[s], m_recv.at[s]) for s in range(4)]
    for copy in lon_copies:
        copy.start()
    for s in (0, 1):
        @pl.when(lat_has[s])
        def _(s=s):
            lat_copies[s].start()
    for copy in q_copies[0:2]:
        copy.start()
    for s in (0, 1):
        @pl.when(lat_has[s])
        def _(s=s):
            q_copies[2 + s].start()

        @pl.when(jnp.logical_not(lat_has[1 - s]))
        def _(s=s):
            latgot[s] = jnp.zeros_like(latgot[s])
            mgot[2 + s] = jnp.zeros_like(mgot[2 + s])
            qgot[2 + s] = jnp.full((qs.shape[0], qs.shape[1]), FAR, F32)

    own = pl.ds(pl.multiple_of(lat * per, per), per)
    got[own] = tsend[own]

    lane_s = lax.broadcasted_iota(jnp.int32, (slots, cells), 1).astype(F32)
    lane_r = lax.broadcasted_iota(jnp.int32, (slots, rows), 1).astype(F32)
    q_rows = q_spread[:, 0:rows]
    hot_w = one(q_rows == lane_r * cells).astype(BF16)
    hot_e = one(q_rows == lane_r * cells + (cells - 1)).astype(BF16)
    hot_n = one(q_spread == lane_s).astype(BF16)
    hot_s = one(q_spread == lane_s + float((rows - 1) * cells)).astype(BF16)
    lane_i = lax.broadcasted_iota(jnp.int32, (1, width), 1).astype(F32)
    lane_ch = jnp.floor((lane_i + 0.5) * (1.0 / ncls))
    lane_cls = lane_i - lane_ch * ncls
    sub_k = lax.broadcasted_iota(jnp.int32, (LANES, width), 0).astype(F32)
    at_obs = one(sub_k == lane_ch).astype(BF16)
    at_wgt = one(sub_k == lane_ch + float(chp)).astype(BF16)
    at_obs = jnp.concatenate([at_obs, at_obs], axis=0)
    at_wgt = jnp.concatenate([at_wgt, at_wgt], axis=0)

    loads[7].wait()
    for copy in lon_copies:
        copy.wait_recv()
    halo = dot(hot_e, longot[0, 0:rows, 0:levels], NN)
    halo += dot(hot_w, longot[1, rows : 2 * rows, 0:levels], NN)
    for copy in t_copies:
        copy.wait_recv()
    told = got[...]
    thi, tlo = split(told)
    told2 = jnp.concatenate([thi, tlo], axis=1)
    observed = dot(told2, at_obs, NN)
    weight = dot(told2, at_wgt, NN)
    mine = jnp.broadcast_to(told[:, 2 * chp : 2 * chp + 1], (slots, width)) == lane_cls
    for s in (0, 1):
        @pl.when(lat_has[1 - s])
        def _(s=s):
            lat_copies[s].wait_recv()
    halo += dot(hot_s, latgot[0], NT) + dot(hot_n, latgot[1], NT)
    columns = (picked[0:slots] + scale * (picked[slots : 2 * slots] + halo)).astype(BF16)
    evolved = dot(columns, jac[...], NT)
    spread = jnp.where(mine, weight * (evolved - observed), 0.0).astype(BF16)
    adj = dot(spread, jac[...], NN)
    mhi, mlo = split(scale * adj)
    msend[:, 0:levels] = mhi
    for copy in m_copies[0:2]:
        copy.start()
    for s in (0, 1):
        @pl.when(lat_has[s])
        def _(s=s):
            m_copies[2 + s].start()

    ahi, alo = split(adj)
    total = dot(
        jnp.concatenate([ahi, alo, mhi, mlo], axis=0), jnp.concatenate([hot, hot, lap, lap], axis=0), TN
    )
    for r in range(rows):
        span = pl.ds(r, levels, stride=rows)
        out[span, :] = inc[span, :] + total[:, r * cells : (r + 1) * cells]

    for copy in q_copies[0:2]:
        copy.wait_recv()
    for s in (0, 1):
        @pl.when(lat_has[1 - s])
        def _(s=s):
            q_copies[2 + s].wait_recv()
    q = [jnp.broadcast_to(qgot[i, 0:1, :], (LANES, qs.shape[1])).T[0:slots] for i in range(4)]
    nearby = []
    for r in range(rows):
        lane, here = cell_iota(slots, cells, r)
        zero = jnp.zeros((slots, cells), F32)
        nearby.append(
            jnp.concatenate(
                [
                    one((here == q[0] + (cells - 1.0)) & (lane == cells - 1.0)),
                    one((here == q[1] - (cells - 1.0)) & (lane == 0.0)),
                    one(lane == q[2]) if r == rows - 1 else zero,
                    one(lane == q[3] - float(cells * (rows - 1))) if r == 0 else zero,
                ],
                axis=0,
            ).astype(BF16)
        )
    nearby = jnp.concatenate(nearby, axis=1)
    for copy in m_copies[0:2]:
        copy.wait_recv()
    for s in (0, 1):
        @pl.when(lat_has[1 - s])
        def _(s=s):
            m_copies[2 + s].wait_recv()
    total = dot(jnp.concatenate([mgot[i, :, 0:levels] for i in range(4)], axis=0), nearby, TN)
    for r in range(rows):
        span = pl.ds(r, levels, stride=rows)
        out[span, :] += total[:, r * cells : (r + 1) * cells]

    for copy in t_copies + lon_copies + q_copies[0:2] + m_copies[0:2]:
        copy.wait_send()
    for s in (0, 1):
        @pl.when(lat_has[s])
        def _(s=s):
            lat_copies[s].wait_send()
            q_copies[2 + s].wait_send()
            m_copies[2 + s].wait_send()


def round_up(x, m):
    return -(-x // m) * m


def on_device(n_lon, n_lat, increment, mixing, mixing_mask, jacobian, fp_col, fp_class, obs, obs_weight):
    nvar, lev, rows, cells = increment.shape
    levels = nvar * lev
    ncls, ch, _ = jacobian.shape
    slots = fp_col.shape[-1]
    chp = round_up(ch, 16)
    dims = (n_lon, n_lat, levels, rows, cells, slots, ncls, ch, chp)
    qwide = round_up(slots, LANES)
    wide = round_up(levels, LANES)
    args = (
        increment.reshape(levels * rows, cells),
        jnp.transpose(jacobian, (1, 0, 2)).reshape(ch * ncls, levels),
        mixing,
        mixing_mask,
        fp_col[0],
        fp_class[0],
        obs.transpose(2, 0, 1, 3).reshape(ch, 1, slots),
        obs_weight.transpose(2, 0, 1, 3).reshape(ch, 1, slots),
    )
    dma = pltpu.SemaphoreType.DMA
    out = pl.pallas_call(
        functools.partial(columns_kernel, dims),
        out_shape=jax.ShapeDtypeStruct((levels * rows, cells), F32),
        in_specs=[pl.BlockSpec(memory_space=pltpu.MemorySpace.HBM)] * len(args),
        out_specs=pl.BlockSpec(memory_space=pltpu.VMEM),
        scratch_shapes=[pltpu.VMEM(a.shape, a.dtype) for a in args]
        + [
            pltpu.VMEM((LANES, qwide), F32),
            pltpu.VMEM((slots, LANES), F32),
            pltpu.VMEM((slots, LANES), F32),
            pltpu.VMEM((8, qwide), F32),
            pltpu.VMEM((4, 8, qwide), F32),
            pltpu.VMEM((2 * rows, wide), BF16),
            pltpu.VMEM((2, 2 * rows, wide), BF16),
            pltpu.VMEM((2, levels, cells), BF16),
            pltpu.VMEM((2, levels, cells), BF16),
            pltpu.VMEM((slots, wide), BF16),
            pltpu.VMEM((4, slots, wide), BF16),
            dma((len(args),)),
            dma((n_lat - 1,)),
            dma((n_lat - 1,)),
        ]
        + [dma((n,)) for n in (2, 2, 2, 2, 4, 4, 4, 4)],
        compiler_params=pltpu.CompilerParams(
            collective_id=0, has_side_effects=True, vmem_limit_bytes=VMEM_LIMIT
        ),
        name="columns",
    )(*[pltpu.with_memory_space_constraint(a, pltpu.MemorySpace.HBM) for a in args])
    return out.reshape(increment.shape)


def solution(mesh):
    return jax.shard_map(
        functools.partial(on_device, mesh.shape["lon"], mesh.shape["lat"]),
        mesh=mesh,
        in_specs=(
            P(None, None, "lat", "lon"),
            P(),
            P("lat", "lon"),
            P(),
            P("lon", "lat", None),
            P("lon", "lat", None),
            P("lon", "lat", None, None),
            P("lon", "lat", None, None),
        ),
        out_specs=P(None, None, "lat", "lon"),
        check_vma=False,
    )
```

```python
import functools

import jax
import jax.numpy as jnp
from jax import lax
from jax.experimental import pallas as pl
from jax.experimental.pallas import tpu as pltpu
from jax.sharding import PartitionSpec as P

MESH = pl.DeviceIdType.MESH
F32 = jnp.float32
BF16 = jnp.bfloat16
FAR = -1.0e6
NT = (((1,), (1,)), ((), ()))
NN = (((1,), (0,)), ((), ()))
TN = (((0,), (0,)), ((), ()))
LANES = 128
VMEM_LIMIT = 40 << 20


def dot(a, b, dims):
    return lax.dot_general(a, b, dims, preferred_element_type=F32)


def split(x):
    hi = x.astype(BF16)
    return hi, (x - hi.astype(F32)).astype(BF16)


def one(cond):
    return jnp.where(cond, 1.0, 0.0)


def cell_iota(slots, cells, row):
    lane = lax.broadcasted_iota(jnp.int32, (slots, cells), 1).astype(F32)
    return lane, lane + float(row * cells)


def laplace_row(q, slots, cells, row):
    lane, here = cell_iota(slots, cells, row)
    out = jnp.where(here == q, -4.0, 0.0)
    out += one((here == q + cells) | (here == q - cells))
    out += one((here == q + 1.0) & (lane != 0.0))
    out += one((here == q - 1.0) & (lane != cells - 1.0))
    return out


def columns_kernel(
    dims,
    inc_hbm, jac_hbm, mixing_hbm, mask_hbm, col_hbm, cls_hbm, obs_hbm, wgt_hbm,
    out, sent_ref, nearby_ref,
    inc, jac, mixing, mask, col, cls_in, obs, wgt,
    xs, tsend, got, qs, qgot, lonsend, longot, latsend, latgot, msend, mgot,
    load_sem, t_send, t_recv, lon_send, lon_recv, lat_send, lat_recv, q_send, q_recv, m_send, m_recv,
):
    n_lon, n_lat, levels, rows, cells, slots, ncls, ch, chp = dims
    lon, lat = lax.axis_index("lon"), lax.axis_index("lat")
    per = slots // n_lat
    width = ncls * ch
    west, east = lax.rem(lon + n_lon - 1, n_lon), lax.rem(lon + 1, n_lon)
    lat_has = (lat > 0, lat < n_lat - 1)
    lat_peer = (jnp.maximum(lat - 1, 0), jnp.minimum(lat + 1, n_lat - 1))

    loads = [
        pltpu.make_async_copy(a, b, load_sem.at[i])
        for i, (a, b) in enumerate(
            (
                (inc_hbm, inc), (col_hbm, col), (cls_hbm, cls_in), (obs_hbm, obs),
                (wgt_hbm, wgt), (mask_hbm, mask), (mixing_hbm, mixing), (jac_hbm, jac),
            )
        )
    ]
    barrier = pltpu.get_barrier_semaphore()
    for k in range(1, n_lat):
        pl.semaphore_signal(
            barrier, inc=1, device_id={"lat": lax.rem(lat + k, n_lat)}, device_id_type=MESH
        )
    for side in (west, east):
        pl.semaphore_signal(barrier, inc=1, device_id={"lon": side}, device_id_type=MESH)
    for load in loads:
        load.start()

    for load in loads[1:7]:
        load.wait()
    xs[...] = jnp.zeros_like(xs)
    xs[0:ch, 0:slots] = obs[:, 0, :]
    xs[chp : chp + ch, 0:slots] = wgt[:, 0, :]
    xs[2 * chp : 2 * chp + 1, 0:slots] = cls_in[...].astype(F32)
    tsend[...] = xs[...].T[0:slots]
    qs[...] = jnp.full_like(qs, FAR)
    q_row = col[...].astype(F32)
    qs[0:1, 0:slots] = jnp.where(q_row < 0.0, FAR, q_row)
    q_spread = jnp.broadcast_to(qs[0:1, :], (LANES, qs.shape[1])).T[0:slots]

    onehots, laps, edge_w, edge_e = [], [], [], []
    sub = lax.broadcasted_iota(jnp.int32, (rows, cells), 0)
    lane8 = lax.broadcasted_iota(jnp.int32, (rows, cells), 1)
    mask_f = jnp.zeros((slots, cells), F32)
    for r in range(rows):
        _, here = cell_iota(slots, cells, r)
        hot = one(here == q_spread)
        mask_f += hot * mask[r : r + 1, :].astype(F32)
        onehots.append(hot)
        laps.append(laplace_row(q_spread, slots, cells, r))
        edge_w.append(one((sub == r) & (lane8 == 0)))
        edge_e.append(one((sub == r) & (lane8 == cells - 1)))
    mask_f = jnp.sum(mask_f, axis=1, keepdims=True)
    hot, lap = (jnp.concatenate(part, axis=1).astype(BF16) for part in (onehots, laps))
    edges = jnp.concatenate(
        [jnp.concatenate(part, axis=1) for part in (edge_w, edge_e)], axis=0
    ).astype(BF16)
    mix_row = jnp.concatenate([mixing[0:1, :], mixing[1:2, :]], axis=1)
    scale = mix_row * mask_f

    loads[0].wait()
    latsend[0] = inc[pl.ds(0, levels, stride=rows), :].astype(BF16)
    latsend[1] = inc[pl.ds(rows - 1, levels, stride=rows), :].astype(BF16)
    field = jnp.concatenate([inc[pl.ds(r, levels, stride=rows), :] for r in range(rows)], axis=1)
    hi, lo = split(field)
    picked = dot(jnp.concatenate([hot, lap, edges], axis=0), hi, NT)
    lonsend[:, 0:levels] = picked[2 * slots :].astype(BF16)

    pl.semaphore_wait(barrier, 2 + n_lat - 1)

    t_copies = []
    for k in range(1, n_lat):
        s = lax.rem(lat + k, n_lat)
        copy = pltpu.make_async_remote_copy(
            src_ref=tsend.at[pl.ds(pl.multiple_of(s * per, per), per)],
            dst_ref=got.at[pl.ds(pl.multiple_of(lat * per, per), per)],
            send_sem=t_send.at[k - 1], recv_sem=t_recv.at[k - 1],
            device_id={"lat": s}, device_id_type=MESH,
        )
        copy.start()
        t_copies.append(copy)

    def to(peer, src, dst, ss, rs):
        return pltpu.make_async_remote_copy(
            src_ref=src, dst_ref=dst, send_sem=ss, recv_sem=rs, device_id=peer, device_id_type=MESH
        )

    peers = ({"lon": west}, {"lon": east}, {"lat": lat_peer[0]}, {"lat": lat_peer[1]})
    lon_copies = [to(peers[s], lonsend, longot.at[s], lon_send.at[s], lon_recv.at[s]) for s in (0, 1)]
    lat_copies = [to(peers[2 + s], latsend.at[s], latgot.at[s], lat_send.at[s], lat_recv.at[s]) for s in (0, 1)]
    q_copies = [to(peers[s], qs, qgot.at[s], q_send.at[s], q_recv.at[s]) for s in range(4)]
    m_copies = [to(peers[s], msend, mgot.at[s], m_send.at[s], m_recv.at[s]) for s in range(4)]
    for copy in lon_copies:
        copy.start()
    for s in (0, 1):
        @pl.when(lat_has[s])
        def _(s=s):
            lat_copies[s].start()
    for copy in q_copies[0:2]:
        copy.start()
    for s in (0, 1):
        @pl.when(lat_has[s])
        def _(s=s):
            q_copies[2 + s].start()

        @pl.when(jnp.logical_not(lat_has[1 - s]))
        def _(s=s):
            latgot[s] = jnp.zeros_like(latgot[s])
            mgot[2 + s] = jnp.zeros_like(mgot[2 + s])
            qgot[2 + s] = jnp.full((qs.shape[0], qs.shape[1]), FAR, F32)

    picked = picked[0 : 2 * slots] + dot(jnp.concatenate([hot, lap], axis=0), lo, NT)
    own = pl.ds(pl.multiple_of(lat * per, per), per)
    got[own] = tsend[own]

    lane_s = lax.broadcasted_iota(jnp.int32, (slots, cells), 1).astype(F32)
    lane_r = lax.broadcasted_iota(jnp.int32, (slots, rows), 1).astype(F32)
    q_rows = q_spread[:, 0:rows]
    hot_w = one(q_rows == lane_r * cells).astype(BF16)
    hot_e = one(q_rows == lane_r * cells + (cells - 1)).astype(BF16)
    hot_n = one(q_spread == lane_s).astype(BF16)
    hot_s = one(q_spread == lane_s + float((rows - 1) * cells)).astype(BF16)
    lane_i = lax.broadcasted_iota(jnp.int32, (1, width), 1).astype(F32)
    lane_ch = jnp.floor((lane_i + 0.5) * (1.0 / ncls))
    lane_cls = lane_i - lane_ch * ncls
    sub_k = lax.broadcasted_iota(jnp.int32, (LANES, width), 0).astype(F32)
    at_obs = one(sub_k == lane_ch).astype(BF16)
    at_wgt = one(sub_k == lane_ch + float(chp)).astype(BF16)
    at_obs = jnp.concatenate([at_obs, at_obs], axis=0)
    at_wgt = jnp.concatenate([at_wgt, at_wgt], axis=0)

    loads[7].wait()
    for copy in lon_copies:
        copy.wait_recv()
    halo = dot(hot_e, longot[0, 0:rows, 0:levels], NN)
    halo += dot(hot_w, longot[1, rows : 2 * rows, 0:levels], NN)
    for copy in t_copies:
        copy.wait_recv()
    told = got[...]
    thi, tlo = split(told)
    told2 = jnp.concatenate([thi, tlo], axis=1)
    observed = dot(told2, at_obs, NN)
    weight = dot(told2, at_wgt, NN)
    mine = jnp.broadcast_to(told[:, 2 * chp : 2 * chp + 1], (slots, width)) == lane_cls
    for s in (0, 1):
        @pl.when(lat_has[1 - s])
        def _(s=s):
            lat_copies[s].wait_recv()
    halo += dot(hot_s, latgot[0], NT) + dot(hot_n, latgot[1], NT)
    columns = (picked[0:slots] + scale * (picked[slots : 2 * slots] + halo)).astype(BF16)
    evolved = dot(columns, jac[...], NT)
    spread = jnp.where(mine, weight * (evolved - observed), 0.0).astype(BF16)
    adj = dot(spread, jac[...], NN)
    mhi, mlo = split(scale * adj)
    msend[:, 0:levels] = mhi
    for copy in m_copies[0:2]:
        copy.start()
    for s in (0, 1):
        @pl.when(lat_has[s])
        def _(s=s):
            m_copies[2 + s].start()

    ahi, alo = split(adj)
    total = dot(
        jnp.concatenate([ahi, alo, mhi, mlo], axis=0), jnp.concatenate([hot, hot, lap, lap], axis=0), TN
    )
    for r in range(rows):
        span = pl.ds(r, levels, stride=rows)
        out[span, :] = inc[span, :] + total[:, r * cells : (r + 1) * cells]

    for copy in q_copies[0:2]:
        copy.wait_recv()
    for s in (0, 1):
        @pl.when(lat_has[1 - s])
        def _(s=s):
            q_copies[2 + s].wait_recv()
    q = [jnp.broadcast_to(qgot[i, 0:1, :], (LANES, qs.shape[1])).T[0:slots] for i in range(4)]
    nearby = []
    for r in range(rows):
        lane, here = cell_iota(slots, cells, r)
        zero = jnp.zeros((slots, cells), F32)
        nearby.append(
            jnp.concatenate(
                [
                    one((here == q[0] + (cells - 1.0)) & (lane == cells - 1.0)),
                    one((here == q[1] - (cells - 1.0)) & (lane == 0.0)),
                    one(lane == q[2]) if r == rows - 1 else zero,
                    one(lane == q[3] - float(cells * (rows - 1))) if r == 0 else zero,
                ],
                axis=0,
            ).astype(BF16)
        )
    nearby_ref[...] = jnp.concatenate(nearby, axis=1)
    for copy in m_copies[0:2]:
        copy.wait_recv()
    for s in (0, 1):
        @pl.when(lat_has[1 - s])
        def _(s=s):
            m_copies[2 + s].wait_recv()
    for i in range(4):
        sent_ref[i * slots : (i + 1) * slots] = mgot[i, :, 0:levels]

    for copy in t_copies + lon_copies + q_copies[0:2] + m_copies[0:2]:
        copy.wait_send()
    for s in (0, 1):
        @pl.when(lat_has[s])
        def _(s=s):
            lat_copies[s].wait_send()
            q_copies[2 + s].wait_send()
            m_copies[2 + s].wait_send()


def gradient_kernel(rows, cells, chunks, part_ref, sent_ref, nearby_ref, out_hbm, out, sems):
    stores = []
    for i, (at, size) in enumerate(chunks):
        total = dot(sent_ref[:, at : at + size], nearby_ref[...], TN)
        for r in range(rows):
            span = pl.ds(at * rows + r, size, stride=rows)
            out[span, :] = part_ref[span, :] + total[:, r * cells : (r + 1) * cells]
        span = pl.ds(at * rows, size * rows)
        stores.append(pltpu.make_async_copy(out.at[span], out_hbm.at[span], sems.at[i]))
        stores[i].start()
    for store in stores:
        store.wait()


def round_up(x, m):
    return -(-x // m) * m


def on_device(n_lon, n_lat, increment, mixing, mixing_mask, jacobian, fp_col, fp_class, obs, obs_weight):
    nvar, lev, rows, cells = increment.shape
    levels = nvar * lev
    ncls, ch, _ = jacobian.shape
    slots = fp_col.shape[-1]
    chp = round_up(ch, 16)
    dims = (n_lon, n_lat, levels, rows, cells, slots, ncls, ch, chp)
    qwide = round_up(slots, LANES)
    wide = round_up(levels, LANES)
    args = (
        increment.reshape(levels * rows, cells),
        jnp.transpose(jacobian, (1, 0, 2)).reshape(ch * ncls, levels),
        mixing,
        mixing_mask,
        fp_col[0],
        fp_class[0],
        obs.transpose(2, 0, 1, 3).reshape(ch, 1, slots),
        obs_weight.transpose(2, 0, 1, 3).reshape(ch, 1, slots),
    )
    dma = pltpu.SemaphoreType.DMA
    vmem = pl.BlockSpec(memory_space=pltpu.VMEM)
    partial = pl.pallas_call(
        functools.partial(columns_kernel, dims),
        out_shape=(
            jax.ShapeDtypeStruct((levels * rows, cells), F32),
            jax.ShapeDtypeStruct((4 * slots, levels), BF16),
            jax.ShapeDtypeStruct((4 * slots, rows * cells), BF16),
        ),
        in_specs=[pl.BlockSpec(memory_space=pltpu.MemorySpace.HBM)] * len(args),
        out_specs=(vmem, vmem, vmem),
        scratch_shapes=[pltpu.VMEM(a.shape, a.dtype) for a in args]
        + [
            pltpu.VMEM((LANES, qwide), F32),
            pltpu.VMEM((slots, LANES), F32),
            pltpu.VMEM((slots, LANES), F32),
            pltpu.VMEM((8, qwide), F32),
            pltpu.VMEM((4, 8, qwide), F32),
            pltpu.VMEM((2 * rows, wide), BF16),
            pltpu.VMEM((2, 2 * rows, wide), BF16),
            pltpu.VMEM((2, levels, cells), BF16),
            pltpu.VMEM((2, levels, cells), BF16),
            pltpu.VMEM((slots, wide), BF16),
            pltpu.VMEM((4, slots, wide), BF16),
            dma((len(args),)),
            dma((n_lat - 1,)),
            dma((n_lat - 1,)),
        ]
        + [dma((n,)) for n in (2, 2, 2, 2, 4, 4, 4, 4)],
        compiler_params=pltpu.CompilerParams(
            collective_id=0, has_side_effects=True, vmem_limit_bytes=VMEM_LIMIT
        ),
        name="columns",
    )(*[pltpu.with_memory_space_constraint(a, pltpu.MemorySpace.HBM) for a in args])
    chunks = [(at, min(LANES, levels - at)) for at in range(0, levels, LANES)]
    out = pl.pallas_call(
        functools.partial(gradient_kernel, rows, cells, chunks),
        out_shape=jax.ShapeDtypeStruct((levels * rows, cells), F32),
        in_specs=[vmem] * 3,
        out_specs=pl.BlockSpec(memory_space=pl.ANY),
        scratch_shapes=[pltpu.VMEM((levels * rows, cells), F32), dma((len(chunks),))],
        compiler_params=pltpu.CompilerParams(vmem_limit_bytes=VMEM_LIMIT),
        name="gradient",
    )(*partial)
    return out.reshape(increment.shape)


def solution(mesh):
    return jax.shard_map(
        functools.partial(on_device, mesh.shape["lon"], mesh.shape["lat"]),
        mesh=mesh,
        in_specs=(
            P(None, None, "lat", "lon"),
            P(),
            P("lat", "lon"),
            P(),
            P("lon", "lat", None),
            P("lon", "lat", None),
            P("lon", "lat", None, None),
            P("lon", "lat", None, None),
        ),
        out_specs=P(None, None, "lat", "lon"),
        check_vma=False,
    )
```

```python
import functools

import jax
import jax.numpy as jnp
from jax import lax
from jax.experimental import pallas as pl
from jax.experimental.pallas import tpu as pltpu
from jax.sharding import PartitionSpec as P

MESH = pl.DeviceIdType.MESH
F32 = jnp.float32
BF16 = jnp.bfloat16
FAR = -1.0e6
NT = (((1,), (1,)), ((), ()))
NN = (((1,), (0,)), ((), ()))
TN = (((0,), (0,)), ((), ()))
LANES = 128
VMEM_LIMIT = 40 << 20


def dot(a, b, dims):
    return lax.dot_general(a, b, dims, preferred_element_type=F32)


def split(x):
    hi = x.astype(BF16)
    return hi, (x - hi.astype(F32)).astype(BF16)


def one(cond):
    return jnp.where(cond, 1.0, 0.0)


def cell_iota(slots, cells, row):
    lane = lax.broadcasted_iota(jnp.int32, (slots, cells), 1).astype(F32)
    return lane, lane + float(row * cells)


def laplace_row(q, slots, cells, row):
    lane, here = cell_iota(slots, cells, row)
    out = jnp.where(here == q, -4.0, 0.0)
    out += one((here == q + cells) | (here == q - cells))
    out += one((here == q + 1.0) & (lane != 0.0))
    out += one((here == q - 1.0) & (lane != cells - 1.0))
    return out


def columns_kernel(
    dims,
    inc_hbm, jac_hbm, mixing_hbm, mask_hbm, col_hbm, cls_hbm, obs_hbm, wgt_hbm,
    out, sent_ref, nearby_ref,
    inc, jac, mixing, mask, col, cls_in, obs, wgt,
    xs, tsend, got, qs, qgot, lonsend, longot, latsend, latgot, msend, mgot,
    load_sem, t_send, t_recv, lon_send, lon_recv, lat_send, lat_recv, q_send, q_recv, m_send, m_recv,
):
    n_lon, n_lat, levels, rows, cells, slots, ncls, ch, chp = dims
    lon, lat = lax.axis_index("lon"), lax.axis_index("lat")
    per = slots // n_lat
    width = ncls * ch
    west, east = lax.rem(lon + n_lon - 1, n_lon), lax.rem(lon + 1, n_lon)
    lat_has = (lat > 0, lat < n_lat - 1)
    lat_peer = (jnp.maximum(lat - 1, 0), jnp.minimum(lat + 1, n_lat - 1))

    loads = [
        pltpu.make_async_copy(a, b, load_sem.at[i])
        for i, (a, b) in enumerate(
            (
                (inc_hbm, inc), (col_hbm, col), (cls_hbm, cls_in), (obs_hbm, obs),
                (wgt_hbm, wgt), (mask_hbm, mask), (mixing_hbm, mixing), (jac_hbm, jac),
            )
        )
    ]
    barrier = pltpu.get_barrier_semaphore()
    for k in range(1, n_lat):
        pl.semaphore_signal(
            barrier, inc=1, device_id={"lat": lax.rem(lat + k, n_lat)}, device_id_type=MESH
        )
    for side in (west, east):
        pl.semaphore_signal(barrier, inc=1, device_id={"lon": side}, device_id_type=MESH)
    for load in loads:
        load.start()

    for load in loads[1:7]:
        load.wait()
    xs[...] = jnp.zeros_like(xs)
    xs[0:ch, 0:slots] = obs[:, 0, :]
    xs[chp : chp + ch, 0:slots] = wgt[:, 0, :]
    xs[2 * chp : 2 * chp + 1, 0:slots] = cls_in[...].astype(F32)
    tsend[...] = xs[...].T[0:slots]
    qs[...] = jnp.full_like(qs, FAR)
    q_row = col[...].astype(F32)
    qs[0:1, 0:slots] = jnp.where(q_row < 0.0, FAR, q_row)
    q_spread = jnp.broadcast_to(qs[0:1, :], (LANES, qs.shape[1])).T[0:slots]

    onehots, laps, edge_w, edge_e = [], [], [], []
    sub = lax.broadcasted_iota(jnp.int32, (rows, cells), 0)
    lane8 = lax.broadcasted_iota(jnp.int32, (rows, cells), 1)
    mask_f = jnp.zeros((slots, cells), F32)
    for r in range(rows):
        _, here = cell_iota(slots, cells, r)
        hot = one(here == q_spread)
        mask_f += hot * mask[r : r + 1, :].astype(F32)
        onehots.append(hot)
        laps.append(laplace_row(q_spread, slots, cells, r))
        edge_w.append(one((sub == r) & (lane8 == 0)))
        edge_e.append(one((sub == r) & (lane8 == cells - 1)))
    mask_f = jnp.sum(mask_f, axis=1, keepdims=True)
    hot, lap = (jnp.concatenate(part, axis=1).astype(BF16) for part in (onehots, laps))
    edges = jnp.concatenate(
        [jnp.concatenate(part, axis=1) for part in (edge_w, edge_e)], axis=0
    ).astype(BF16)
    mix_row = jnp.concatenate([mixing[0:1, :], mixing[1:2, :]], axis=1)
    scale = mix_row * mask_f

    loads[0].wait()
    latsend[0] = inc[pl.ds(0, levels, stride=rows), :].astype(BF16)
    latsend[1] = inc[pl.ds(rows - 1, levels, stride=rows), :].astype(BF16)
    pl.semaphore_wait(barrier, 2 + n_lat - 1)

    t_copies = []
    for k in range(1, n_lat):
        s = lax.rem(lat + k, n_lat)
        copy = pltpu.make_async_remote_copy(
            src_ref=tsend.at[pl.ds(pl.multiple_of(s * per, per), per)],
            dst_ref=got.at[pl.ds(pl.multiple_of(lat * per, per), per)],
            send_sem=t_send.at[k - 1], recv_sem=t_recv.at[k - 1],
            device_id={"lat": s}, device_id_type=MESH,
        )
        copy.start()
        t_copies.append(copy)

    def to(peer, src, dst, ss, rs):
        return pltpu.make_async_remote_copy(
            src_ref=src, dst_ref=dst, send_sem=ss, recv_sem=rs, device_id=peer, device_id_type=MESH
        )

    peers = ({"lon": west}, {"lon": east}, {"lat": lat_peer[0]}, {"lat": lat_peer[1]})
    lon_copies = [to(peers[s], lonsend, longot.at[s], lon_send.at[s], lon_recv.at[s]) for s in (0, 1)]
    lat_copies = [to(peers[2 + s], latsend.at[s], latgot.at[s], lat_send.at[s], lat_recv.at[s]) for s in (0, 1)]
    q_copies = [to(peers[s], qs, qgot.at[s], q_send.at[s], q_recv.at[s]) for s in range(4)]
    m_copies = [to(peers[s], msend, mgot.at[s], m_send.at[s], m_recv.at[s]) for s in range(4)]
    for s in (0, 1):
        @pl.when(lat_has[s])
        def _(s=s):
            lat_copies[s].start()
    for copy in q_copies[0:2]:
        copy.start()
    for s in (0, 1):
        @pl.when(lat_has[s])
        def _(s=s):
            q_copies[2 + s].start()

        @pl.when(jnp.logical_not(lat_has[1 - s]))
        def _(s=s):
            latgot[s] = jnp.zeros_like(latgot[s])
            mgot[2 + s] = jnp.zeros_like(mgot[2 + s])
            qgot[2 + s] = jnp.full((qs.shape[0], qs.shape[1]), FAR, F32)

    field = jnp.concatenate([inc[pl.ds(r, levels, stride=rows), :] for r in range(rows)], axis=1)
    hi, lo = split(field)
    picked = dot(jnp.concatenate([hot, lap, edges], axis=0), hi, NT)
    lonsend[:, 0:levels] = picked[2 * slots :].astype(BF16)
    for copy in lon_copies:
        copy.start()
    picked = picked[0 : 2 * slots] + dot(jnp.concatenate([hot, lap], axis=0), lo, NT)
    own = pl.ds(pl.multiple_of(lat * per, per), per)
    got[own] = tsend[own]

    lane_s = lax.broadcasted_iota(jnp.int32, (slots, cells), 1).astype(F32)
    lane_r = lax.broadcasted_iota(jnp.int32, (slots, rows), 1).astype(F32)
    q_rows = q_spread[:, 0:rows]
    hot_w = one(q_rows == lane_r * cells).astype(BF16)
    hot_e = one(q_rows == lane_r * cells + (cells - 1)).astype(BF16)
    hot_n = one(q_spread == lane_s).astype(BF16)
    hot_s = one(q_spread == lane_s + float((rows - 1) * cells)).astype(BF16)
    lane_i = lax.broadcasted_iota(jnp.int32, (1, width), 1).astype(F32)
    lane_ch = jnp.floor((lane_i + 0.5) * (1.0 / ncls))
    lane_cls = lane_i - lane_ch * ncls
    sub_k = lax.broadcasted_iota(jnp.int32, (2 * chp, width), 0).astype(F32)
    at_obs = one(sub_k == lane_ch).astype(BF16)
    at_wgt = one(sub_k == lane_ch + float(chp)).astype(BF16)

    loads[7].wait()
    for copy in t_copies:
        copy.wait_recv()
    told = got[...]
    thi, tlo = split(told)
    told2 = jnp.concatenate([thi, tlo], axis=0)[:, 0 : 2 * chp]
    observed = dot(told2, at_obs, NN)
    observed = observed[0:slots] + observed[slots:]
    weight = dot(told2, at_wgt, NN)
    weight = weight[0:slots] + weight[slots:]
    mine = jnp.broadcast_to(told[:, 2 * chp : 2 * chp + 1], (slots, width)) == lane_cls
    for s in (0, 1):
        @pl.when(lat_has[1 - s])
        def _(s=s):
            lat_copies[s].wait_recv()
    halo = dot(hot_s, latgot[0], NT) + dot(hot_n, latgot[1], NT)
    for copy in lon_copies:
        copy.wait_recv()
    halo += dot(hot_e, longot[0, 0:rows, 0:levels], NN)
    halo += dot(hot_w, longot[1, rows : 2 * rows, 0:levels], NN)
    columns = (picked[0:slots] + scale * (picked[slots : 2 * slots] + halo)).astype(BF16)
    evolved = dot(columns, jac[...], NT)
    spread = jnp.where(mine, weight * (evolved - observed), 0.0).astype(BF16)
    adj = dot(spread, jac[...], NN)
    mhi, mlo = split(scale * adj)
    msend[:, 0:levels] = mhi
    for copy in m_copies[0:2]:
        copy.start()
    for s in (0, 1):
        @pl.when(lat_has[s])
        def _(s=s):
            m_copies[2 + s].start()

    ahi, alo = split(adj)
    total = dot(
        jnp.concatenate([ahi, alo, mhi, mlo], axis=0), jnp.concatenate([hot, hot, lap, lap], axis=0), TN
    )
    for r in range(rows):
        span = pl.ds(r, levels, stride=rows)
        out[span, :] = inc[span, :] + total[:, r * cells : (r + 1) * cells]

    for copy in q_copies[0:2]:
        copy.wait_recv()
    for s in (0, 1):
        @pl.when(lat_has[1 - s])
        def _(s=s):
            q_copies[2 + s].wait_recv()
    q = [jnp.broadcast_to(qgot[i, 0:1, :], (LANES, qs.shape[1])).T[0:slots] for i in range(4)]
    nearby = []
    for r in range(rows):
        lane, here = cell_iota(slots, cells, r)
        zero = jnp.zeros((slots, cells), F32)
        nearby.append(
            jnp.concatenate(
                [
                    one((here == q[0] + (cells - 1.0)) & (lane == cells - 1.0)),
                    one((here == q[1] - (cells - 1.0)) & (lane == 0.0)),
                    one(lane == q[2]) if r == rows - 1 else zero,
                    one(lane == q[3] - float(cells * (rows - 1))) if r == 0 else zero,
                ],
                axis=0,
            ).astype(BF16)
        )
    nearby_ref[...] = jnp.concatenate(nearby, axis=1)
    for copy in m_copies[0:2]:
        copy.wait_recv()
    for s in (0, 1):
        @pl.when(lat_has[1 - s])
        def _(s=s):
            m_copies[2 + s].wait_recv()
    for i in range(4):
        sent_ref[i * slots : (i + 1) * slots] = mgot[i, :, 0:levels]

    for copy in t_copies + lon_copies + q_copies[0:2] + m_copies[0:2]:
        copy.wait_send()
    for s in (0, 1):
        @pl.when(lat_has[s])
        def _(s=s):
            lat_copies[s].wait_send()
            q_copies[2 + s].wait_send()
            m_copies[2 + s].wait_send()


def gradient_kernel(rows, cells, chunks, part_ref, sent_ref, nearby_ref, out_hbm, out, sems):
    stores = []
    for i, (at, size) in enumerate(chunks):
        total = dot(sent_ref[:, at : at + size], nearby_ref[...], TN)
        for r in range(rows):
            span = pl.ds(at * rows + r, size, stride=rows)
            out[span, :] = part_ref[span, :] + total[:, r * cells : (r + 1) * cells]
        span = pl.ds(at * rows, size * rows)
        stores.append(pltpu.make_async_copy(out.at[span], out_hbm.at[span], sems.at[i]))
        stores[i].start()
    for store in stores:
        store.wait()


def round_up(x, m):
    return -(-x // m) * m


def on_device(n_lon, n_lat, increment, mixing, mixing_mask, jacobian, fp_col, fp_class, obs, obs_weight):
    nvar, lev, rows, cells = increment.shape
    levels = nvar * lev
    ncls, ch, _ = jacobian.shape
    slots = fp_col.shape[-1]
    chp = round_up(ch, 16)
    dims = (n_lon, n_lat, levels, rows, cells, slots, ncls, ch, chp)
    qwide = round_up(slots, LANES)
    wide = round_up(levels, LANES)
    args = (
        increment.reshape(levels * rows, cells),
        jnp.transpose(jacobian, (1, 0, 2)).reshape(ch * ncls, levels),
        mixing,
        mixing_mask,
        fp_col[0],
        fp_class[0],
        obs.transpose(2, 0, 1, 3).reshape(ch, 1, slots),
        obs_weight.transpose(2, 0, 1, 3).reshape(ch, 1, slots),
    )
    dma = pltpu.SemaphoreType.DMA
    vmem = pl.BlockSpec(memory_space=pltpu.VMEM)
    partial = pl.pallas_call(
        functools.partial(columns_kernel, dims),
        out_shape=(
            jax.ShapeDtypeStruct((levels * rows, cells), F32),
            jax.ShapeDtypeStruct((4 * slots, levels), BF16),
            jax.ShapeDtypeStruct((4 * slots, rows * cells), BF16),
        ),
        in_specs=[pl.BlockSpec(memory_space=pltpu.MemorySpace.HBM)] * len(args),
        out_specs=(vmem, vmem, vmem),
        scratch_shapes=[pltpu.VMEM(a.shape, a.dtype) for a in args]
        + [
            pltpu.VMEM((LANES, qwide), F32),
            pltpu.VMEM((slots, LANES), F32),
            pltpu.VMEM((slots, LANES), F32),
            pltpu.VMEM((8, qwide), F32),
            pltpu.VMEM((4, 8, qwide), F32),
            pltpu.VMEM((2 * rows, wide), BF16),
            pltpu.VMEM((2, 2 * rows, wide), BF16),
            pltpu.VMEM((2, levels, cells), BF16),
            pltpu.VMEM((2, levels, cells), BF16),
            pltpu.VMEM((slots, wide), BF16),
            pltpu.VMEM((4, slots, wide), BF16),
            dma((len(args),)),
            dma((n_lat - 1,)),
            dma((n_lat - 1,)),
        ]
        + [dma((n,)) for n in (2, 2, 2, 2, 4, 4, 4, 4)],
        compiler_params=pltpu.CompilerParams(
            collective_id=0, has_side_effects=True, vmem_limit_bytes=VMEM_LIMIT
        ),
        name="columns",
    )(*[pltpu.with_memory_space_constraint(a, pltpu.MemorySpace.HBM) for a in args])
    chunks = [(at, min(LANES, levels - at)) for at in range(0, levels, LANES)]
    out = pl.pallas_call(
        functools.partial(gradient_kernel, rows, cells, chunks),
        out_shape=jax.ShapeDtypeStruct((levels * rows, cells), F32),
        in_specs=[vmem] * 3,
        out_specs=pl.BlockSpec(memory_space=pl.ANY),
        scratch_shapes=[pltpu.VMEM((levels * rows, cells), F32), dma((len(chunks),))],
        compiler_params=pltpu.CompilerParams(vmem_limit_bytes=VMEM_LIMIT),
        name="gradient",
    )(*partial)
    return out.reshape(increment.shape)


def solution(mesh):
    return jax.shard_map(
        functools.partial(on_device, mesh.shape["lon"], mesh.shape["lat"]),
        mesh=mesh,
        in_specs=(
            P(None, None, "lat", "lon"),
            P(),
            P("lat", "lon"),
            P(),
            P("lon", "lat", None),
            P("lon", "lat", None),
            P("lon", "lat", None, None),
            P("lon", "lat", None, None),
        ),
        out_specs=P(None, None, "lat", "lon"),
        check_vma=False,
    )
```

```python
import functools

import jax
import jax.numpy as jnp
from jax import lax
from jax.experimental import pallas as pl
from jax.experimental.pallas import tpu as pltpu
from jax.sharding import PartitionSpec as P

MESH = pl.DeviceIdType.MESH
F32 = jnp.float32
BF16 = jnp.bfloat16
FAR = -1.0e6
NT = (((1,), (1,)), ((), ()))
NN = (((1,), (0,)), ((), ()))
TN = (((0,), (0,)), ((), ()))
LANES = 128
VMEM_LIMIT = 40 << 20


def dot(a, b, dims):
    return lax.dot_general(a, b, dims, preferred_element_type=F32)


def split(x):
    hi = x.astype(BF16)
    return hi, (x - hi.astype(F32)).astype(BF16)


def one(cond):
    return jnp.where(cond, 1.0, 0.0)


def cell_iota(slots, cells, row):
    lane = lax.broadcasted_iota(jnp.int32, (slots, cells), 1).astype(F32)
    return lane, lane + float(row * cells)


def laplace_row(q, slots, cells, row):
    lane, here = cell_iota(slots, cells, row)
    out = jnp.where(here == q, -4.0, 0.0)
    out += one((here == q + cells) | (here == q - cells))
    out += one((here == q + 1.0) & (lane != 0.0))
    out += one((here == q - 1.0) & (lane != cells - 1.0))
    return out


def columns_kernel(
    dims,
    inc_hbm, jac_hbm, mixing_hbm, mask_hbm, col_hbm, cls_hbm, obs_hbm, wgt_hbm,
    out, sent_ref, nearby_ref,
    inc, jac, mixing, mask, col, cls_in, obs, wgt,
    xs, tsend, got, qs, qgot, lonsend, longot, latsend, latgot, msend, mgot,
    load_sem, t_send, t_recv, lon_send, lon_recv, lat_send, lat_recv, q_send, q_recv, m_send, m_recv,
):
    n_lon, n_lat, levels, rows, cells, slots, ncls, ch, chp = dims
    lon, lat = lax.axis_index("lon"), lax.axis_index("lat")
    per = slots // n_lat
    width = ncls * ch
    west, east = lax.rem(lon + n_lon - 1, n_lon), lax.rem(lon + 1, n_lon)
    lat_has = (lat > 0, lat < n_lat - 1)
    lat_peer = (jnp.maximum(lat - 1, 0), jnp.minimum(lat + 1, n_lat - 1))

    loads = [
        pltpu.make_async_copy(a, b, load_sem.at[i])
        for i, (a, b) in enumerate(
            (
                (inc_hbm, inc), (col_hbm, col), (cls_hbm, cls_in), (obs_hbm, obs),
                (wgt_hbm, wgt), (mask_hbm, mask), (mixing_hbm, mixing), (jac_hbm, jac),
            )
        )
    ]
    barrier = pltpu.get_barrier_semaphore()
    for k in range(1, n_lat):
        pl.semaphore_signal(
            barrier, inc=1, device_id={"lat": lax.rem(lat + k, n_lat)}, device_id_type=MESH
        )
    for side in (west, east):
        pl.semaphore_signal(barrier, inc=1, device_id={"lon": side}, device_id_type=MESH)
    for load in loads:
        load.start()

    for load in loads[1:7]:
        load.wait()
    xs[...] = jnp.zeros_like(xs)
    xs[0:ch, 0:slots] = obs[:, 0, :]
    xs[chp : chp + ch, 0:slots] = wgt[:, 0, :]
    xs[2 * chp : 2 * chp + 1, 0:slots] = cls_in[...].astype(F32)
    tsend[...] = xs[...].T[0:slots]
    qs[...] = jnp.full_like(qs, FAR)
    q_row = col[...].astype(F32)
    qs[0:1, 0:slots] = jnp.where(q_row < 0.0, FAR, q_row)
    q_spread = jnp.broadcast_to(qs[0:1, :], (LANES, qs.shape[1])).T[0:slots]

    onehots, laps, edge_w, edge_e = [], [], [], []
    sub = lax.broadcasted_iota(jnp.int32, (rows, cells), 0)
    lane8 = lax.broadcasted_iota(jnp.int32, (rows, cells), 1)
    mask_f = jnp.zeros((slots, cells), F32)
    for r in range(rows):
        _, here = cell_iota(slots, cells, r)
        hot = one(here == q_spread)
        mask_f += hot * mask[r : r + 1, :].astype(F32)
        onehots.append(hot)
        laps.append(laplace_row(q_spread, slots, cells, r))
        edge_w.append(one((sub == r) & (lane8 == 0)))
        edge_e.append(one((sub == r) & (lane8 == cells - 1)))
    mask_f = jnp.sum(mask_f, axis=1, keepdims=True)
    hot, lap = (jnp.concatenate(part, axis=1).astype(BF16) for part in (onehots, laps))
    edges = jnp.concatenate(
        [jnp.concatenate(part, axis=1) for part in (edge_w, edge_e)], axis=0
    ).astype(BF16)
    mix_row = jnp.concatenate([mixing[0:1, :], mixing[1:2, :]], axis=1)
    scale = mix_row * mask_f

    loads[0].wait()
    latsend[0] = inc[pl.ds(0, levels, stride=rows), :].astype(BF16)
    latsend[1] = inc[pl.ds(rows - 1, levels, stride=rows), :].astype(BF16)
    field = jnp.concatenate([inc[pl.ds(r, levels, stride=rows), :] for r in range(rows)], axis=1)
    hi, lo = split(field)
    picked = dot(jnp.concatenate([hot, lap, edges], axis=0), hi, NT)
    lonsend[:, 0:levels] = picked[2 * slots :].astype(BF16)
    pl.semaphore_wait(barrier, 2 + n_lat - 1)

    t_copies = []
    for k in range(1, n_lat):
        s = lax.rem(lat + k, n_lat)
        copy = pltpu.make_async_remote_copy(
            src_ref=tsend.at[pl.ds(pl.multiple_of(s * per, per), per)],
            dst_ref=got.at[pl.ds(pl.multiple_of(lat * per, per), per)],
            send_sem=t_send.at[k - 1], recv_sem=t_recv.at[k - 1],
            device_id={"lat": s}, device_id_type=MESH,
        )
        copy.start()
        t_copies.append(copy)

    def to(peer, src, dst, ss, rs):
        return pltpu.make_async_remote_copy(
            src_ref=src, dst_ref=dst, send_sem=ss, recv_sem=rs, device_id=peer, device_id_type=MESH
        )

    peers = ({"lon": west}, {"lon": east}, {"lat": lat_peer[0]}, {"lat": lat_peer[1]})
    lon_copies = [to(peers[s], lonsend, longot.at[s], lon_send.at[s], lon_recv.at[s]) for s in (0, 1)]
    lat_copies = [to(peers[2 + s], latsend.at[s], latgot.at[s], lat_send.at[s], lat_recv.at[s]) for s in (0, 1)]
    q_copies = [to(peers[s], qs, qgot.at[s], q_send.at[s], q_recv.at[s]) for s in range(4)]
    m_copies = [to(peers[s], msend, mgot.at[s], m_send.at[s], m_recv.at[s]) for s in range(4)]
    for copy in lon_copies:
        copy.start()
    for s in (0, 1):
        @pl.when(lat_has[s])
        def _(s=s):
            lat_copies[s].start()
    for copy in q_copies[0:2]:
        copy.start()
    for s in (0, 1):
        @pl.when(lat_has[s])
        def _(s=s):
            q_copies[2 + s].start()

        @pl.when(jnp.logical_not(lat_has[1 - s]))
        def _(s=s):
            latgot[s] = jnp.zeros_like(latgot[s])
            mgot[2 + s] = jnp.zeros_like(mgot[2 + s])
            qgot[2 + s] = jnp.full((qs.shape[0], qs.shape[1]), FAR, F32)

    picked = picked[0 : 2 * slots] + dot(jnp.concatenate([hot, lap], axis=0), lo, NT)
    own = pl.ds(pl.multiple_of(lat * per, per), per)
    got[own] = tsend[own]

    lane_s = lax.broadcasted_iota(jnp.int32, (slots, cells), 1).astype(F32)
    lane_r = lax.broadcasted_iota(jnp.int32, (slots, rows), 1).astype(F32)
    q_rows = q_spread[:, 0:rows]
    hot_w = one(q_rows == lane_r * cells).astype(BF16)
    hot_e = one(q_rows == lane_r * cells + (cells - 1)).astype(BF16)
    hot_n = one(q_spread == lane_s).astype(BF16)
    hot_s = one(q_spread == lane_s + float((rows - 1) * cells)).astype(BF16)
    lane_i = lax.broadcasted_iota(jnp.int32, (1, width), 1).astype(F32)
    lane_ch = jnp.floor((lane_i + 0.5) * (1.0 / ncls))
    lane_cls = lane_i - lane_ch * ncls
    sub_k = lax.broadcasted_iota(jnp.int32, (2 * chp, width), 0).astype(F32)
    at_obs = one(sub_k == lane_ch).astype(BF16)
    at_wgt = one(sub_k == lane_ch + float(chp)).astype(BF16)

    loads[7].wait()
    for copy in t_copies:
        copy.wait_recv()
    told = got[...]
    thi, tlo = split(told)
    told2 = jnp.concatenate([thi, tlo], axis=0)[:, 0 : 2 * chp]
    observed = dot(told2, at_obs, NN)
    observed = observed[0:slots] + observed[slots:]
    weight = dot(told2, at_wgt, NN)
    weight = weight[0:slots] + weight[slots:]
    mine = jnp.broadcast_to(told[:, 2 * chp : 2 * chp + 1], (slots, width)) == lane_cls
    for s in (0, 1):
        @pl.when(lat_has[1 - s])
        def _(s=s):
            lat_copies[s].wait_recv()
    halo = dot(hot_s, latgot[0], NT) + dot(hot_n, latgot[1], NT)
    for copy in lon_copies:
        copy.wait_recv()
    halo += dot(hot_e, longot[0, 0:rows, 0:levels], NN)
    halo += dot(hot_w, longot[1, rows : 2 * rows, 0:levels], NN)
    columns = (picked[0:slots] + scale * (picked[slots : 2 * slots] + halo)).astype(BF16)
    evolved = dot(columns, jac[...], NT)
    spread = jnp.where(mine, weight * (evolved - observed), 0.0).astype(BF16)
    adj = dot(spread, jac[...], NN)
    mhi, mlo = split(scale * adj)
    msend[:, 0:levels] = mhi
    for copy in m_copies[0:2]:
        copy.start()
    for s in (0, 1):
        @pl.when(lat_has[s])
        def _(s=s):
            m_copies[2 + s].start()

    ahi, alo = split(adj)
    total = dot(
        jnp.concatenate([ahi, alo, mhi, mlo], axis=0), jnp.concatenate([hot, hot, lap, lap], axis=0), TN
    )
    for r in range(rows):
        span = pl.ds(r, levels, stride=rows)
        out[span, :] = inc[span, :] + total[:, r * cells : (r + 1) * cells]

    for copy in q_copies[0:2]:
        copy.wait_recv()
    for s in (0, 1):
        @pl.when(lat_has[1 - s])
        def _(s=s):
            q_copies[2 + s].wait_recv()
    q = [jnp.broadcast_to(qgot[i, 0:1, :], (LANES, qs.shape[1])).T[0:slots] for i in range(4)]
    nearby = []
    for r in range(rows):
        lane, here = cell_iota(slots, cells, r)
        zero = jnp.zeros((slots, cells), F32)
        nearby.append(
            jnp.concatenate(
                [
                    one((here == q[0] + (cells - 1.0)) & (lane == cells - 1.0)),
                    one((here == q[1] - (cells - 1.0)) & (lane == 0.0)),
                    one(lane == q[2]) if r == rows - 1 else zero,
                    one(lane == q[3] - float(cells * (rows - 1))) if r == 0 else zero,
                ],
                axis=0,
            ).astype(BF16)
        )
    nearby_ref[...] = jnp.concatenate(nearby, axis=1)
    for copy in m_copies[0:2]:
        copy.wait_recv()
    for s in (0, 1):
        @pl.when(lat_has[1 - s])
        def _(s=s):
            m_copies[2 + s].wait_recv()
    for i in range(4):
        sent_ref[i * slots : (i + 1) * slots] = mgot[i, :, 0:levels]

    for copy in t_copies + lon_copies + q_copies[0:2] + m_copies[0:2]:
        copy.wait_send()
    for s in (0, 1):
        @pl.when(lat_has[s])
        def _(s=s):
            lat_copies[s].wait_send()
            q_copies[2 + s].wait_send()
            m_copies[2 + s].wait_send()


def gradient_kernel(rows, cells, chunks, part_ref, sent_ref, nearby_ref, out_hbm, out, sems):
    stores = []
    for i, (at, size) in enumerate(chunks):
        total = dot(sent_ref[:, at : at + size], nearby_ref[...], TN)
        for r in range(rows):
            span = pl.ds(at * rows + r, size, stride=rows)
            out[span, :] = part_ref[span, :] + total[:, r * cells : (r + 1) * cells]
        span = pl.ds(at * rows, size * rows)
        stores.append(pltpu.make_async_copy(out.at[span], out_hbm.at[span], sems.at[i]))
        stores[i].start()
    for store in stores:
        store.wait()


def round_up(x, m):
    return -(-x // m) * m


def on_device(n_lon, n_lat, increment, mixing, mixing_mask, jacobian, fp_col, fp_class, obs, obs_weight):
    nvar, lev, rows, cells = increment.shape
    levels = nvar * lev
    ncls, ch, _ = jacobian.shape
    slots = fp_col.shape[-1]
    chp = round_up(ch, 16)
    dims = (n_lon, n_lat, levels, rows, cells, slots, ncls, ch, chp)
    qwide = round_up(slots, LANES)
    wide = round_up(levels, LANES)
    args = (
        increment.reshape(levels * rows, cells),
        jnp.transpose(jacobian, (1, 0, 2)).reshape(ch * ncls, levels),
        mixing,
        mixing_mask,
        fp_col[0],
        fp_class[0],
        obs.transpose(2, 0, 1, 3).reshape(ch, 1, slots),
        obs_weight.transpose(2, 0, 1, 3).reshape(ch, 1, slots),
    )
    dma = pltpu.SemaphoreType.DMA
    vmem = pl.BlockSpec(memory_space=pltpu.VMEM)
    partial = pl.pallas_call(
        functools.partial(columns_kernel, dims),
        out_shape=(
            jax.ShapeDtypeStruct((levels * rows, cells), F32),
            jax.ShapeDtypeStruct((4 * slots, levels), BF16),
            jax.ShapeDtypeStruct((4 * slots, rows * cells), BF16),
        ),
        in_specs=[pl.BlockSpec(memory_space=pltpu.MemorySpace.HBM)] * len(args),
        out_specs=(vmem, vmem, vmem),
        scratch_shapes=[pltpu.VMEM(a.shape, a.dtype) for a in args]
        + [
            pltpu.VMEM((LANES, qwide), F32),
            pltpu.VMEM((slots, LANES), F32),
            pltpu.VMEM((slots, LANES), F32),
            pltpu.VMEM((8, qwide), F32),
            pltpu.VMEM((4, 8, qwide), F32),
            pltpu.VMEM((2 * rows, wide), BF16),
            pltpu.VMEM((2, 2 * rows, wide), BF16),
            pltpu.VMEM((2, levels, cells), BF16),
            pltpu.VMEM((2, levels, cells), BF16),
            pltpu.VMEM((slots, wide), BF16),
            pltpu.VMEM((4, slots, wide), BF16),
            dma((len(args),)),
            dma((n_lat - 1,)),
            dma((n_lat - 1,)),
        ]
        + [dma((n,)) for n in (2, 2, 2, 2, 4, 4, 4, 4)],
        compiler_params=pltpu.CompilerParams(
            collective_id=0, has_side_effects=True, vmem_limit_bytes=VMEM_LIMIT
        ),
        name="columns",
    )(*[pltpu.with_memory_space_constraint(a, pltpu.MemorySpace.HBM) for a in args])
    chunks = [(at, min(LANES, levels - at)) for at in range(0, levels, LANES)]
    out = pl.pallas_call(
        functools.partial(gradient_kernel, rows, cells, chunks),
        out_shape=jax.ShapeDtypeStruct((levels * rows, cells), F32),
        in_specs=[vmem] * 3,
        out_specs=pl.BlockSpec(memory_space=pl.ANY),
        scratch_shapes=[pltpu.VMEM((levels * rows, cells), F32), dma((len(chunks),))],
        compiler_params=pltpu.CompilerParams(vmem_limit_bytes=VMEM_LIMIT),
        name="gradient",
    )(*partial)
    return out.reshape(increment.shape)


def solution(mesh):
    return jax.shard_map(
        functools.partial(on_device, mesh.shape["lon"], mesh.shape["lat"]),
        mesh=mesh,
        in_specs=(
            P(None, None, "lat", "lon"),
            P(),
            P("lat", "lon"),
            P(),
            P("lon", "lat", None),
            P("lon", "lat", None),
            P("lon", "lat", None, None),
            P("lon", "lat", None, None),
        ),
        out_specs=P(None, None, "lat", "lon"),
        check_vma=False,
    )
```
